256 devices in a mesh: face: 32 (over y_hi, z, core), level: 4 (over x), ens: 2 (over y_lo).
Axes of the slice: x: 4, y: 4 (y_hi: 2, y_lo: 2; y = y_hi * 2 + y_lo), z: 8, core: 2. Of those that a mesh axis runs over, the one named last changes fastest.
Arguments:
- state: bfloat16 [256, 16, 16, 512], P(('ens', 'face'), None, None, 'level'), parts along dimension 0, may hold values from -6 to 6
- conv_weight: bfloat16 [2, 2, 9, 64, 64], replicated, may hold values from -0.25 to 0.25
- mix_in: bfloat16 [2, 512, 512], replicated, may hold values from -0.25 to 0.25
- mix_out: bfloat16 [2, 512, 512], replicated, may hold values from -0.25 to 0.25
- edge_source: int32 [128, 4], replicated, may hold values from 0 to 511, as said below
- corner_source: int32 [128, 4], replicated, may hold values from -1 to 511, as said below
Outputs:
- forecast: bfloat16 [256, 16, 16, 512], P(('ens', 'face'), None, None, 'level'), parts along dimension 0
The draws below stay inside these ranges and needn't reach their ends.
There are 2 independent parts, one for each index of `ens`. The reference program is written for one: setup_inputs(seed, part) draws one part's arguments, and reference() takes and returns one part's arrays. A program takes and returns all parts, laid end to end along the dimension named above; an argument that names none is the same for every part. Nothing has to cross between parts.
Inputs may be any that keep to these rules, and one draw needn't show every extreme that they name: Each strip number 0 to 511 appears exactly once. Tiles 4 d to 4 d + 3 lie on index d of face; the tile u of edge_source[t, s] lies on the device of t, on the device whose index differs from it in the lowest bit, or on the device two indices away in either direction (cyclically). Exactly 4 strips of one device border tiles of the device whose index differs in the lowest bit; when 32 > 4 exactly 2 border tiles of a device two indices away. `corner_source`: each entry is -1 or a corner pixel number; a corner pixel number appears at most once. Its tile lies on a device allowed for edge_source, or on a device two indices (cyclically) away from the one whose index differs from t's device in the lowest bit.
All inputs are finite; a program needn't handle non-finite values.
Results may differ from the reference program's by a relative error of at most 0.022.
Values may be sent and summed in bfloat16 or wider, within the bound.
No kernel may reach another device: no remote copies, remote signals or barrier semaphores. Data moves between devices by JAX's collectives and lax.ppermute only.
A program may use at most 64 MiB of HBM per device.

```python
import jax
import jax.numpy as jnp

C = 64
HID = 512
P_SIZE = 16
BLOCKS = 2
TILES = 128
LEVELS = 8


def tile_graph(key):
    graph_key = jax.random.fold_in(key, 7)
    key_perm, key_rot, key_missing = jax.random.split(graph_key, 3)
    device_count = TILES // 4
    columns = device_count
    orders = jax.vmap(lambda single: jax.random.permutation(single, 4))(jax.random.split(key_perm, device_count))
    grid_rows = jnp.broadcast_to(jnp.arange(4, dtype=jnp.int32)[:, None], (4, columns))
    grid_cols = jnp.broadcast_to(jnp.arange(columns, dtype=jnp.int32)[None, :], (4, columns))
    holder = grid_cols // 2 * 2 + grid_rows // 2
    position = grid_rows % 2 * 2 + grid_cols % 2
    tile_at = (holder * 4 + orders[holder, position]).astype(jnp.int32)
    flat_tiles = tile_at.reshape(-1)
    row_of = jnp.zeros((TILES,), jnp.int32).at[flat_tiles].set(grid_rows.reshape(-1))
    col_of = jnp.zeros((TILES,), jnp.int32).at[flat_tiles].set(grid_cols.reshape(-1))
    rotation = jax.random.randint(key_rot, (TILES,), 0, 4).astype(jnp.int32)
    side_ids = jnp.arange(4, dtype=jnp.int32)[None, :]
    grid_side = (side_ids + rotation[:, None]) % 4
    side_row = jnp.array([-1, 0, 1, 0], jnp.int32)
    side_col = jnp.array([0, 1, 0, -1], jnp.int32)
    near_row = (row_of[:, None] + side_row[grid_side]) % 4
    near_col = (col_of[:, None] + side_col[grid_side]) % columns
    facing = tile_at[near_row, near_col]
    edge_ids = facing * 4 + (grid_side + 2 - rotation[facing]) % 4
    corner_row = jnp.array([-1, -1, 1, 1], jnp.int32)
    corner_col = jnp.array([-1, 1, 1, -1], jnp.int32)
    diag_row = (row_of[:, None] + corner_row[grid_side]) % 4
    diag_col = (col_of[:, None] + corner_col[grid_side]) % columns
    diagonal = tile_at[diag_row, diag_col]
    corner_ids = diagonal * 4 + (grid_side + 2 - rotation[diagonal]) % 4
    missing = jax.random.randint(key_missing, (TILES, 4), 0, 4) == 0
    missing = missing & (corner_ids != 4 * TILES - 1) | (corner_ids == 0)
    corner_ids = jnp.where(missing, -1, corner_ids)
    return (edge_ids.astype(jnp.int32), corner_ids.astype(jnp.int32))


def draw_edge_source(key, part):
    return tile_graph(key)[0]


def draw_corner_source(key, part):
    return tile_graph(key)[1]


def steps_of(key, extent, cuts, smallest, top_value):
    loudness, own = 1.0, jax.random.fold_in(key, 6)
    for dim, blocks in cuts:
        draws = jnp.exp(jax.random.uniform(jax.random.fold_in(own, dim), (blocks,), jnp.float32, smallest / len(cuts), top_value / len(cuts)))
        loudness = loudness * jnp.repeat(draws, extent[dim] // blocks).reshape([-1 if axis == dim else 1 for axis in range(len(extent))])
    return loudness


def gaussian(rng, shape, spread, limit, cuts=(), held_as=jnp.bfloat16):
    gain = steps_of(rng, shape, cuts, -0.22, 0.18) if cuts else 1.0
    values = jax.random.normal(rng, shape, jnp.float32) * spread * gain
    return jnp.minimum(jnp.maximum(values, -limit), limit).astype(held_as)


def setup_inputs(seed: int = 0, part: int = 0) -> dict:
    arg_keys = jax.random.split(jax.random.key(seed), 7)
    part_keys = jax.random.split(jax.random.fold_in(arg_keys[6], part), 7)
    state = gaussian(part_keys[0], (TILES, P_SIZE, P_SIZE, LEVELS * C), 1.0, 6.0, ((0, 32), (3, 4)))
    conv_weight = gaussian(arg_keys[1], (BLOCKS, 2, 9, C, C), (9 * C) ** -0.5, 0.25)
    mix_in = gaussian(arg_keys[2], (BLOCKS, LEVELS * C, HID), (LEVELS * C) ** -0.5, 0.25)
    mix_out = gaussian(arg_keys[3], (BLOCKS, HID, LEVELS * C), HID ** -0.5, 0.25)
    edge_source = draw_edge_source(jax.random.fold_in(arg_keys[6], 71), part)
    corner_source = draw_corner_source(jax.random.fold_in(arg_keys[6], 71), part)
    return dict(state=state, conv_weight=conv_weight, mix_in=mix_in, mix_out=mix_out, edge_source=edge_source, corner_source=corner_source)


def export_edges(field):
    north = field[:, 0, :, :]
    east = field[:, :, -1, :]
    south = field[:, -1, ::-1, :]
    west = field[:, ::-1, 0, :]
    strips = jnp.stack([north, east, south, west], 1)
    corners = jnp.stack([field[:, 0, 0], field[:, 0, -1], field[:, -1, -1], field[:, -1, 0]], 1)
    return strips, corners


def assemble(field, rim_strips, corner_vals):
    north = rim_strips[:, 0, ::-1]
    east = rim_strips[:, 1, ::-1]
    south = rim_strips[:, 2]
    west = rim_strips[:, 3]
    upper = jnp.concatenate([corner_vals[:, 0:1], north, corner_vals[:, 1:2]], 1)
    lower = jnp.concatenate([corner_vals[:, 3:4], south, corner_vals[:, 2:3]], 1)
    middle = jnp.concatenate([west[:, :, None], field, east[:, :, None]], 2)
    return jnp.concatenate([upper[:, None], middle, lower[:, None]], 1)


def pad_tiles(field, edge_source, corner_source):
    strips, corners = export_edges(field)
    features = field.shape[-1]
    strip_rows = strips.reshape(TILES * 4, P_SIZE, features)
    rim_strips = strip_rows[edge_source.reshape(-1)].reshape(TILES, 4, P_SIZE, features)
    corner_rows = corners.reshape(TILES * 4, features)
    corner_index = jnp.maximum(corner_source, 0).reshape(-1)
    present = (corner_source >= 0).astype(field.dtype)[..., None]
    corner_vals = corner_rows[corner_index].reshape(TILES, 4, features) * present
    return assemble(field, rim_strips, corner_vals)


def convolve(padded, weight):
    total = jnp.zeros((TILES * P_SIZE * P_SIZE * LEVELS, C), jnp.float32)
    for row_off in range(3):
        for col_off in range(3):
            window = padded[:, row_off:row_off + P_SIZE, col_off:col_off + P_SIZE, :].reshape(-1, C)
            total = total + jnp.dot(window, weight[3 * row_off + col_off], preferred_element_type=jnp.float32)
    return total.reshape(TILES, P_SIZE, P_SIZE, LEVELS * C)


def reference(state, conv_weight, mix_in, mix_out, edge_source, corner_source):
    field = state
    for block in range(BLOCKS):
        inner = jax.nn.gelu(convolve(pad_tiles(field, edge_source, corner_source), conv_weight[block, 0])).astype(jnp.bfloat16)
        field = (field.astype(jnp.float32) + convolve(pad_tiles(inner, edge_source, corner_source), conv_weight[block, 1])).astype(jnp.bfloat16)
        column_rows = field.reshape(-1, LEVELS * C)
        hidden = jax.nn.gelu(jnp.dot(column_rows, mix_in[block], preferred_element_type=jnp.float32)).astype(jnp.bfloat16)
        mixed = jnp.dot(hidden, mix_out[block], preferred_element_type=jnp.float32)
        field = (field.astype(jnp.float32) + mixed.reshape(field.shape)).astype(jnp.bfloat16)
    return field
```

```python
import functools

import jax
import jax.numpy as jnp
import numpy as np
from jax import lax
from jax.experimental import pallas as pl
from jax.experimental.pallas import tpu as pltpu
from jax.sharding import PartitionSpec as P

BF16, F32, I32 = jnp.bfloat16, jnp.float32, jnp.int32
SIDE = 16
PIXELS = SIDE * SIDE
HERE = 4
STRIPS = 4 * HERE
ZERO_ROW = 6 * STRIPS
VMEM_LIMIT = 48 * 1024 * 1024


def one_hot(columns, width):
    table = np.zeros((len(columns), width), np.float32)
    for row, column in enumerate(columns):
        table[row, column] = 1.0
    return table.astype(jnp.bfloat16)


def strip_table():
    rising, falling = range(SIDE), range(SIDE - 1, -1, -1)
    last = SIDE - 1
    return one_hot(
        [k for k in rising]
        + [k * SIDE + last for k in rising]
        + [last * SIDE + k for k in falling]
        + [k * SIDE for k in falling],
        PIXELS,
    )


def corner_table():
    return one_hot([SIDE * strip for strip in range(STRIPS)], SIDE * STRIPS)


def shift_table():
    half, rim = SIDE // 2, PIXELS // 2
    groups = []
    for group in range(2):
        columns = []
        for i in range(half):
            for j in range(SIDE):
                columns.append(i * SIDE + j - 1 if j else rim + 48 + group * half + i)
        for i in range(half):
            for j in range(SIDE):
                columns.append(i * SIDE + j + 1 if j < SIDE - 1 else rim + 16 + SIDE - 1 - group * half - i)
        groups.append(one_hot(columns, rim + 80))
    return np.stack(groups)


def cap_table():
    last, columns = SIDE - 1, []
    columns += [64 if j == 0 else last - (j - 1) for j in range(SIDE)]
    columns += [67 if j == 0 else 32 + j - 1 for j in range(SIDE)]
    columns += [last - j for j in range(SIDE)]
    columns += [32 + j for j in range(SIDE)]
    columns += [65 if j == last else last - (j + 1) for j in range(SIDE)]
    columns += [66 if j == last else 32 + j + 1 for j in range(SIDE)]
    return one_hot(columns, 80)


def dot(a, b):
    return jnp.dot(a, b, preferred_element_type=F32)


def gelu(z):
    return 0.5 * z * (1.0 + jnp.tanh(0.7978845608028654 * (z + 0.044715 * (z * z * z))))


def export(field_ref, strips_ref, send_ref, up_ref, down_ref, pair_ref, picks_ref, corners_ref):
    features = field_ref.shape[-1]
    for tile in range(HERE):
        strips = dot(picks_ref[...], field_ref[tile].reshape(PIXELS, features)).astype(BF16)
        strips_ref[4 * tile : 4 * tile + 4] = strips.reshape(4, SIDE, features)
    address(strips_ref, send_ref, up_ref, down_ref, pair_ref, corners_ref)


def address(strips_ref, send_ref, up_ref, down_ref, pair_ref, corners_ref):
    features = strips_ref.shape[-1]
    corners = dot(corners_ref[...], strips_ref[...].reshape(STRIPS * SIDE, features)).astype(BF16)
    for slot in range(4):
        pair_ref[slot] = strips_ref[send_ref[slot]]
    for slot in range(2):
        up_ref[slot] = strips_ref[send_ref[4 + slot]]
        down_ref[slot] = strips_ref[send_ref[6 + slot]]
    pair_ref[4] = corners
    up_ref[2] = corners
    down_ref[2] = corners


def first_kernel(faces, field_ref, edge_ref, picks_ref, corners_ref, strips_ref, up_ref, down_ref, pair_ref, table_ref, send_ref):
    own = lax.axis_index("face")
    paired, ahead, behind = own ^ 1, lax.rem(own + 2, faces), lax.rem(own + faces - 2, faces)
    for target, start, capacity in ((paired, 0, 4), (ahead, 4, 2), (behind, 6, 2)):
        taken = jnp.int32(0)
        for strip in range(STRIPS):
            wanted = edge_ref[strip % 4, target * HERE + strip // 4]
            fits = jnp.logical_and(wanted // STRIPS == own, taken < capacity)
            send_ref[jnp.where(fits, start + taken, 8)] = wanted % STRIPS
            taken = taken + fits.astype(I32)
    for slot in range(8):
        table_ref[slot] = send_ref[slot]
    export(field_ref, strips_ref, send_ref, up_ref, down_ref, pair_ref, picks_ref, corners_ref)


def side_kernel(faces, edge_ref, corner_ref, conv_ref, table_ref, narrow1_ref, narrow2_ref, wide1_ref, wide2_ref):
    own = lax.axis_index("face")
    paired, ahead, behind = own ^ 1, lax.rem(own + 2, faces), lax.rem(own + faces - 2, faces)
    from_pair, from_behind, from_ahead = jnp.int32(0), jnp.int32(0), jnp.int32(0)
    for strip in range(STRIPS):
        wanted = edge_ref[strip % 4, own * HERE + strip // 4]
        holder, place = wanted // STRIPS, wanted % STRIPS
        by_pair, by_behind, mine = holder == paired, holder == behind, holder == own
        by_ahead = jnp.logical_not(mine | by_pair | by_behind)
        table_ref[strip] = jnp.where(
            mine,
            place,
            jnp.where(
                by_pair,
                STRIPS + jnp.minimum(from_pair, 3),
                jnp.where(
                    by_behind,
                    STRIPS + 4 + jnp.minimum(from_behind, 1),
                    STRIPS + 6 + jnp.minimum(from_ahead, 1),
                ),
            ),
        )
        from_pair = from_pair + by_pair.astype(I32)
        from_behind = from_behind + by_behind.astype(I32)
        from_ahead = from_ahead + by_ahead.astype(I32)
    for corner in range(STRIPS):
        wanted = corner_ref[corner % 4, own * HERE + corner // 4]
        safe = jnp.maximum(wanted, 0)
        holder, place = safe // STRIPS, safe % STRIPS
        source = jnp.where(
            holder == own,
            0,
            jnp.where(
                holder == paired,
                1,
                jnp.where(holder == behind, 2, jnp.where(holder == (behind ^ 1), 3, jnp.where(holder == ahead, 4, 5))),
            ),
        )
        table_ref[STRIPS + corner] = jnp.where(wanted < 0, ZERO_ROW, source * STRIPS + place)
    for conv, (narrow, wide) in enumerate(((narrow1_ref, wide1_ref), (narrow2_ref, wide2_ref))):
        narrow[...] = jnp.zeros_like(narrow)
        wide[...] = jnp.zeros_like(wide)
        for tap in range(9):
            for level in range(2):
                narrow[pl.ds(128 * tap + 64 * level, 64), pl.ds(64 * level, 64)] = conv_ref[0, conv, tap]
            for level in range(4):
                wide[pl.ds(256 * tap + 64 * level, 64), pl.ds(64 * level, 64)] = conv_ref[1, conv, tap]


def gather_rims(strips_ref, behind_ref, ahead_ref, pair_ref, behind2_ref, ahead2_ref, table_ref, held, corners, row, rims):
    features = strips_ref.shape[-1]
    for strip in range(STRIPS):
        held[strip] = strips_ref[strip]
        corners[strip : strip + 1] = strips_ref[strip, 0:1].astype(F32)
    for slot in range(4):
        held[STRIPS + slot] = pair_ref[slot]
    for slot in range(2):
        held[STRIPS + 4 + slot] = behind_ref[slot]
        held[STRIPS + 6 + slot] = ahead_ref[slot]
    for source, ref in enumerate((pair_ref.at[4], behind_ref.at[2], behind2_ref.at[2], ahead_ref.at[2], ahead2_ref.at[2])):
        corners[(source + 1) * STRIPS : (source + 2) * STRIPS] = ref[...].astype(F32)
    corners[ZERO_ROW : ZERO_ROW + 8] = jnp.zeros((8, features), F32)
    row[...] = jnp.zeros_like(row)
    for tile in range(HERE):
        for side in range(4):
            rims[tile, SIDE * side : SIDE * (side + 1)] = held[table_ref[4 * tile + side]]
            pick = table_ref[STRIPS + 4 * tile + side]
            row[tile, side : side + 1] = corners[pl.ds(pick, 1)]
        rims[tile, 64:80] = row[tile].astype(BF16)


def padded(field_ref, tile, rims, shift_ref, cap_ref, shifted):
    features = field_ref.shape[-1]
    rim = rims[tile]
    caps = dot(cap_ref[...], rim).astype(BF16).reshape(6, SIDE, features)
    for b in range(3):
        shifted[b, 0] = caps[2 * b]
        shifted[b, SIDE + 1] = caps[2 * b + 1]
    half = SIDE // 2
    for group in range(2):
        rows = field_ref[tile, half * group : half * (group + 1)]
        shifted[1, 1 + half * group : 1 + half * (group + 1)] = rows
        known = jnp.concatenate([rows.reshape(half * SIDE, features), rim], 0)
        moved = dot(shift_ref[group], known).astype(BF16).reshape(2, half, SIDE, features)
        shifted[0, 1 + half * group : 1 + half * (group + 1)] = moved[0]
        shifted[2, 1 + half * group : 1 + half * (group + 1)] = moved[1]


def windows(shifted, lanes):
    return jnp.concatenate(
        [shifted[b, a : a + SIDE, :, lanes].reshape(PIXELS, -1) for a in range(3) for b in range(3)], 1
    )


def conv_kernel(last, narrow, *refs):
    field_ref, strips_ref, behind_ref, ahead_ref, pair_ref, behind2_ref, ahead2_ref = refs[:7]
    table_ref, send_ref, weight_ref, shift_ref, cap_ref, picks_ref, corners_ref = refs[7:14]
    rest = list(refs[14:])
    state_ref = rest.pop(0) if last else None
    out_ref, out_strips_ref = rest[:2]
    messages, scratch = (rest[2:5], rest[5:]) if not (last and narrow) else ((), rest[2:])
    held, corners, row, rims, shifted = scratch
    features = field_ref.shape[-1]
    gather_rims(strips_ref, behind_ref, ahead_ref, pair_ref, behind2_ref, ahead2_ref, table_ref, held, corners, row, rims)
    width = weight_ref.shape[-1]
    for tile in range(HERE):
        window = shifted.at[tile]
        padded(field_ref, tile, rims, shift_ref, cap_ref, window)
        for group in range(features // width):
            lanes = slice(width * group, width * (group + 1))
            total = dot(windows(window, lanes), weight_ref[...])
            if last:
                total = total + state_ref[tile, :, :, lanes].reshape(PIXELS, width).astype(F32)
            else:
                total = gelu(total)
            out_ref[tile, :, :, lanes] = total.astype(BF16).reshape(SIDE, SIDE, width)
        strips = dot(picks_ref[...], out_ref[tile].reshape(PIXELS, features)).astype(BF16)
        out_strips_ref[4 * tile : 4 * tile + 4] = strips.reshape(4, SIDE, features)
    if messages:
        up_ref, down_ref, to_pair_ref = messages
        address(out_strips_ref, send_ref, up_ref, down_ref, to_pair_ref, corners_ref)


def mix_rows(block, level, parts, mix_in_ref, mix_out_ref, outs):
    levels = mix_in_ref.shape[1] // 128
    order = [lax.rem(level + levels - back, levels) for back in range(levels)]
    first = jnp.concatenate([mix_in_ref[block, pl.ds(pl.multiple_of(128 * place, 128), 128), :] for place in order], 0)
    hidden = gelu(dot(jnp.concatenate(parts, 1), first)).astype(BF16)
    mixed = []
    for back in range(outs):
        columns = pl.ds(pl.multiple_of(128 * order[back], 128), 128)
        mixed.append((parts[back].astype(F32) + dot(hidden, mix_out_ref[block, :, columns])).astype(BF16))
    return mixed


def mix_strips_kernel(block, own_ref, one_ref, two_ref, three_ref, mix_in_ref, mix_out_ref, send_ref, corners_ref, strips_ref, up_ref, down_ref, pair_ref):
    level = lax.axis_index("level")
    parts = [ref[...].reshape(STRIPS * SIDE, 128) for ref in (own_ref, one_ref, two_ref, three_ref)]
    mixed = jnp.concatenate(mix_rows(block, level, parts, mix_in_ref, mix_out_ref, 4), 1)
    strips_ref[...] = mixed.reshape(STRIPS, SIDE, 512)
    address(strips_ref, send_ref, up_ref, down_ref, pair_ref, corners_ref)


def mix_tiles_kernel(block, own_ref, one_ref, two_ref, three_ref, mix_in_ref, mix_out_ref, out_ref):
    level = lax.axis_index("level")
    for tile in range(HERE):
        parts = [ref[tile].reshape(PIXELS, 128) for ref in (own_ref, one_ref, two_ref, three_ref)]
        mixed = mix_rows(block, level, parts, mix_in_ref, mix_out_ref, 4)
        for back in range(4):
            out_ref[tile, :, :, 128 * back : 128 * (back + 1)] = mixed[back].reshape(SIDE, SIDE, 128)


def final_kernel(block, *refs):
    field_ref, strips_ref, behind_ref, ahead_ref, pair_ref, behind2_ref, ahead2_ref = refs[:7]
    table_ref, weight_ref, shift_ref, cap_ref, state_ref, mix_in_ref, mix_out_ref, out_ref = refs[7:15]
    held, corners, row, rims, shifted = refs[15:]
    level = lax.axis_index("level")
    gather_rims(strips_ref, behind_ref, ahead_ref, pair_ref, behind2_ref, ahead2_ref, table_ref, held, corners, row, rims)
    width = weight_ref.shape[-1]
    for tile in range(HERE):
        window = shifted.at[tile]
        padded(field_ref, tile, rims, shift_ref, cap_ref, window)
        parts = []
        for group in range(field_ref.shape[-1] // width):
            lanes = slice(width * group, width * (group + 1))
            total = dot(windows(window, lanes), weight_ref[...])
            total = (total + state_ref[tile, :, :, lanes].reshape(PIXELS, width).astype(F32)).astype(BF16)
            parts += [total[:, 128 * part : 128 * (part + 1)] for part in range(width // 128)]
        (mixed,) = mix_rows(block, level, parts, mix_in_ref, mix_out_ref, 1)
        out_ref[tile] = mixed.reshape(SIDE, SIDE, 128)


V = pl.BlockSpec(memory_space=pltpu.VMEM)
S = pl.BlockSpec(memory_space=pltpu.SMEM)


def call(kernel, name, in_specs, out_specs, out_shape, scratch, args):
    return pl.pallas_call(
        kernel,
        name=name,
        in_specs=in_specs,
        out_specs=out_specs,
        out_shape=out_shape,
        scratch_shapes=scratch,
        compiler_params=pltpu.CompilerParams(vmem_limit_bytes=VMEM_LIMIT),
    )(*args)


def arrays(*shapes):
    return [jax.ShapeDtypeStruct(shape, BF16) for shape in shapes]


def message_shapes(features):
    return (3, SIDE, features), (3, SIDE, features), (5, SIDE, features)


def halo_scratch(features):
    return [
        pltpu.VMEM((STRIPS + 8, SIDE, features), BF16),
        pltpu.VMEM((ZERO_ROW + 8, features), F32),
        pltpu.VMEM((HERE, SIDE, features), F32),
        pltpu.VMEM((HERE, 80, features), BF16),
        pltpu.VMEM((HERE, 3, SIDE + 2, SIDE, features), BF16),
    ]


def exchange(up, down, to_pair):
    faces = lax.axis_size("face")
    pairs = [(i, i ^ 1) for i in range(faces)]
    behind = lax.ppermute(up, "face", [(i, (i + 2) % faces) for i in range(faces)])
    ahead = lax.ppermute(down, "face", [(i, (i - 2) % faces) for i in range(faces)])
    paired = lax.ppermute(to_pair, "face", pairs)
    return behind, ahead, paired, lax.ppermute(behind, "face", pairs), lax.ppermute(ahead, "face", pairs)


def from_level(shard, distance):
    levels = lax.axis_size("level")
    return lax.ppermute(shard, "level", [(i, (i + distance) % levels) for i in range(levels)])


def shards(state, conv_weight, mix_in, mix_out, edge_source, corner_source):
    faces = lax.axis_size("face")
    features = state.shape[-1]
    wide = 4 * features
    picks, corners, shift, cap = (jnp.asarray(t) for t in (strip_table(), corner_table(), shift_table(), cap_table()))
    edges, cornered = edge_source.T, corner_source.T
    tile_shape, wide_shape = (HERE, SIDE, SIDE, features), (HERE, SIDE, SIDE, wide)
    strip_shape, wide_strips = (STRIPS, SIDE, features), (STRIPS, SIDE, wide)

    strips, up, down, to_pair, send = call(
        functools.partial(first_kernel, faces), "first",
        [V, S, V, V], [V, V, V, V, S],
        arrays(strip_shape, *message_shapes(features)) + [jax.ShapeDtypeStruct((8,), I32)],
        [pltpu.SMEM((16,), I32)],
        (state, edges, picks, corners),
    )
    table, narrow1, narrow2, wide1, wide2 = call(
        functools.partial(side_kernel, faces), "side",
        [S, S, V], [S, V, V, V, V],
        [jax.ShapeDtypeStruct((2 * STRIPS,), I32)] + arrays((1152, 128), (1152, 128), (2304, 256), (2304, 256)),
        [],
        (edges, cornered, conv_weight),
    )

    def conv(last, narrow, field, strips, received, weight, residual):
        size = field.shape[-1]
        shapes = [field.shape, (STRIPS, SIDE, size)] + ([] if last and narrow else list(message_shapes(size)))
        return call(
            functools.partial(conv_kernel, last, narrow), f"conv_{size}_{int(last)}",
            [V] * 7 + [S, S] + [V] * 5 + ([V] if last else []), [V] * len(shapes),
            arrays(*shapes), halo_scratch(size),
            (field, strips, *received, table, send, weight, shift, cap, picks, corners) + ((residual,) if last else ()),
        )

    inner, strips, up, down, to_pair = conv(False, True, state, strips, exchange(up, down, to_pair), narrow1, None)
    field, strips = conv(True, True, inner, strips, exchange(up, down, to_pair), narrow2, state)

    others = [from_level(strips, d) for d in (1, 2, 3)]
    tiles = [from_level(field, d) for d in (1, 2, 3)]
    strips, up, down, to_pair = call(
        functools.partial(mix_strips_kernel, 0), "mix_strips",
        [V] * 6 + [S, V], [V] * 4,
        arrays(wide_strips, *message_shapes(wide)), [],
        (strips, *others, mix_in, mix_out, send, corners),
    )
    received = exchange(up, down, to_pair)
    field = call(
        functools.partial(mix_tiles_kernel, 0), "mix_tiles",
        [V] * 6, V, arrays(wide_shape)[0], [],
        (field, *tiles, mix_in, mix_out),
    )
    inner, strips, up, down, to_pair = conv(False, False, field, strips, received, wide1, None)
    return call(
        functools.partial(final_kernel, 1), "final",
        [V] * 7 + [S] + [V] * 6, V, arrays(tile_shape)[0], halo_scratch(wide),
        (inner, strips, *exchange(up, down, to_pair), table, wide2, shift, cap, field, mix_in, mix_out),
    )


def solution(mesh):
    return jax.shard_map(
        shards,
        mesh=mesh,
        in_specs=(P(("ens", "face"), None, None, "level"), P(), P(), P(), P(), P()),
        out_specs=P(("ens", "face"), None, None, "level"),
        check_vma=False,
    )
```

```python
import functools

import jax
import jax.numpy as jnp
import numpy as np
from jax import lax
from jax.experimental import pallas as pl
from jax.experimental.pallas import tpu as pltpu
from jax.sharding import PartitionSpec as P

BF16, F32, I32 = jnp.bfloat16, jnp.float32, jnp.int32
SIDE = 16
INNER = SIDE - 2
PIXELS = SIDE * SIDE
HERE = 4
STRIPS = 4 * HERE
BORDER = 4 * SIDE
ZERO_ROW = 6 * STRIPS
VMEM_LIMIT = 16 * 1024 * 1024


def one_hot(columns, width):
    table = np.zeros((len(columns), width), np.float32)
    for row, column in enumerate(columns):
        if column is not None:
            table[row, column] = 1.0
    return table.astype(jnp.bfloat16)


def strip_pixel(side, k, depth=0):
    last = SIDE - 1
    return ((depth, k), (k, last - depth), (last - depth, last - k), (last - k, depth))[side]


def ring(depth):
    places = {}
    for side in range(4):
        for k in range(depth, SIDE - depth):
            places.setdefault(strip_pixel(side, k, depth), SIDE * side + k)
    return places


def border_table():
    outer, inner, last = ring(0), ring(1), SIDE - 1
    corner = {(-1, -1): 0, (-1, SIDE): 1, (SIDE, SIDE): 2, (SIDE, -1): 3}
    columns = []
    for a in range(3):
        for b in range(3):
            for side in range(4):
                for k in range(SIDE):
                    i, j = strip_pixel(side, k)
                    i, j = i + a - 1, j + b - 1
                    if (i, j) in corner:
                        columns.append(3 * BORDER + corner[i, j])
                    elif i < 0:
                        columns.append(2 * BORDER + last - j)
                    elif j > last:
                        columns.append(2 * BORDER + SIDE + last - i)
                    elif i > last:
                        columns.append(2 * BORDER + 2 * SIDE + j)
                    elif j < 0:
                        columns.append(2 * BORDER + 3 * SIDE + i)
                    elif (i, j) in outer:
                        columns.append(outer[i, j])
                    else:
                        columns.append(BORDER + inner[i, j])
    return one_hot(columns, 3 * BORDER + SIDE)


def tile_table():
    outer, half = ring(0), INNER // 2
    groups = []
    for group in range(2):
        columns = []
        for b in range(3):
            for i in range(SIDE // 2 * group, SIDE // 2 * (group + 1)):
                for j in range(SIDE):
                    column = j + b - 1
                    if column < 0 or column >= SIDE:
                        columns.append(None)
                    elif (i, column) in outer:
                        columns.append(half * SIDE + outer[i, column])
                    else:
                        columns.append((i - 1 - half * group) * SIDE + column)
        groups.append(one_hot(columns, half * SIDE + BORDER))
    return np.stack(groups)


def inner_table():
    columns = []
    for side in range(4):
        for k in range(SIDE):
            i, j = strip_pixel(side, k, 1)
            columns.append((i - 1) * SIDE + j if 1 <= k < SIDE - 1 else None)
    return one_hot(columns, INNER * SIDE)


def dot(a, b):
    return jnp.dot(a, b, preferred_element_type=F32)


def gelu(z):
    return 0.5 * z * (1.0 + jnp.tanh(0.7978845608028654 * (z + 0.044715 * (z * z * z))))


def copies(sems, *pairs):
    started = [pltpu.make_async_copy(source, target, sems.at[n]) for n, (source, target) in enumerate(pairs)]
    for copy in started:
        copy.start()
    return started


def address(strips_ref, send_ref, near_ref, far_ref, pair_ref, corners_ref):
    features = strips_ref.shape[-1]
    corners = dot(corners_ref[...], strips_ref[...].reshape(STRIPS * SIDE, features)).astype(BF16)
    for slot in range(4):
        pair_ref[slot] = strips_ref[send_ref[slot]]
    for slot in range(2):
        near_ref[slot] = strips_ref[send_ref[4 + slot]]
        far_ref[slot] = strips_ref[send_ref[6 + slot]]
    pair_ref[4] = corners
    near_ref[2] = corners
    far_ref[2] = corners


def neighbours(faces):
    own = lax.axis_index("face")
    ahead, behind = lax.rem(own + 2, faces), lax.rem(own + faces - 2, faces)
    return own, own ^ 1, own ^ 2, jnp.where(own & 2 == 0, behind, ahead)


def first_kernel(faces, state_ref, edge_ref, strips_ref, near_ref, far_ref, pair_ref, table_ref, held_ref, corners_ref, edges, send, sems):
    edge_copy, state_copy = copies(sems, (edge_ref, edges), (state_ref, held_ref))
    row = lax.broadcasted_iota(I32, (BORDER, PIXELS), 0)
    column = lax.broadcasted_iota(I32, (BORDER, PIXELS), 1)
    side, k, last = row // SIDE, row % SIDE, SIDE - 1
    place = jnp.where(
        side == 0,
        k,
        jnp.where(side == 1, k * SIDE + last, jnp.where(side == 2, last * SIDE + last - k, (last - k) * SIDE)),
    )
    picks = (place == column).astype(F32).astype(BF16)
    row = lax.broadcasted_iota(I32, (STRIPS, STRIPS * SIDE), 0)
    column = lax.broadcasted_iota(I32, (STRIPS, STRIPS * SIDE), 1)
    corners_ref[...] = (row * SIDE == column).astype(F32).astype(BF16)
    own, paired, near, far = neighbours(faces)
    edge_copy.wait()
    for target, start, capacity in ((paired, 0, 4), (near, 4, 2), (far, 6, 2)):
        taken = jnp.int32(0)
        for strip in range(STRIPS):
            wanted = edges[strip % 4, target * HERE + strip // 4]
            fits = jnp.logical_and(wanted // STRIPS == own, taken < capacity)
            send[jnp.where(fits, start + taken, 8)] = wanted % STRIPS
            taken = taken + fits.astype(I32)
    for slot in range(8):
        table_ref[slot] = send[slot]
    state_copy.wait()
    features = state_ref.shape[-1]
    for tile in range(HERE):
        strips = dot(picks, held_ref[tile].reshape(PIXELS, features)).astype(BF16)
        strips_ref[4 * tile : 4 * tile + 4] = strips.reshape(4, SIDE, features)
    address(strips_ref, send, near_ref, far_ref, pair_ref, corners_ref)


def side_kernel(faces, *refs):
    edge_ref, corner_ref, conv_ref, border_ref, tile_ref, inner_ref, send_ref, state_ref = refs[:8]
    table_ref, narrow1_ref, narrow2_ref, border_held, tile_held, inner_held, strips_ref = refs[8:15]
    edges, cornered, conv, sems = refs[15:]
    started = copies(
        sems,
        (edge_ref, edges),
        (corner_ref, cornered),
        (conv_ref.at[0], conv),
        (inner_ref, inner_held),
        (border_ref, border_held),
        (tile_ref, tile_held),
    )
    for narrow in (narrow1_ref, narrow2_ref):
        narrow[...] = jnp.zeros_like(narrow)
    own, paired, near, far = neighbours(faces)
    from_pair, from_near, from_far = jnp.int32(0), jnp.int32(0), jnp.int32(0)
    for copy in started[:4]:
        copy.wait()
    for slot in range(8):
        table_ref[2 * STRIPS + slot] = send_ref[slot]
    for strip in range(STRIPS):
        wanted = edges[strip % 4, own * HERE + strip // 4]
        holder, place = wanted // STRIPS, wanted % STRIPS
        by_pair, by_near, mine = holder == paired, holder == near, holder == own
        by_far = jnp.logical_not(mine | by_pair | by_near)
        table_ref[strip] = jnp.where(
            mine,
            place,
            jnp.where(
                by_pair,
                STRIPS + jnp.minimum(from_pair, 3),
                jnp.where(
                    by_near,
                    STRIPS + 4 + jnp.minimum(from_near, 1),
                    STRIPS + 6 + jnp.minimum(from_far, 1),
                ),
            ),
        )
        from_pair = from_pair + by_pair.astype(I32)
        from_near = from_near + by_near.astype(I32)
        from_far = from_far + by_far.astype(I32)
    for corner in range(STRIPS):
        wanted = cornered[corner % 4, own * HERE + corner // 4]
        safe = jnp.maximum(wanted, 0)
        holder, place = safe // STRIPS, safe % STRIPS
        source = jnp.where(
            holder == own,
            0,
            jnp.where(
                holder == paired,
                1,
                jnp.where(holder == near, 2, jnp.where(holder == (near ^ 1), 3, jnp.where(holder == far, 4, 5))),
            ),
        )
        table_ref[STRIPS + corner] = jnp.where(wanted < 0, ZERO_ROW, source * STRIPS + place)
    for layer, narrow in enumerate((narrow1_ref, narrow2_ref)):
        spread(conv, layer, narrow)
    inner_strips(state_ref, 1, inner_held, strips_ref)
    for copy in started[4:]:
        copy.wait()


def spread(conv, layer, weight):
    width = weight.shape[-1]
    for tap in range(9):
        for level in range(width // 64):
            weight[pl.ds(width * tap + 64 * level, 64), pl.ds(64 * level, 64)] = conv[layer, tap]


def weights_kernel(*refs):
    conv_ref, mix_in_ref, mix_out_ref, _, narrow1_ref, narrow2_ref, wide1_ref, wide2_ref, mix_in_held, mix_out_held, conv, sems = refs
    started = copies(sems, (conv_ref.at[1], conv), (mix_in_ref, mix_in_held), (mix_out_ref, mix_out_held))
    for weight in (narrow1_ref, narrow2_ref, wide1_ref, wide2_ref):
        weight[...] = jnp.zeros_like(weight)
    started[0].wait()
    for layer, weights in enumerate(((narrow1_ref, wide1_ref), (narrow2_ref, wide2_ref))):
        for weight in weights:
            spread(conv, layer, weight)
    for copy in started[1:]:
        copy.wait()


def inner_strips(field_ref, top, inner_ref, strips_ref):
    features = field_ref.shape[-1]
    for tile in range(HERE):
        rows = field_ref[tile, top : top + INNER].reshape(INNER * SIDE, features)
        strips = dot(inner_ref[...], rows).astype(BF16)
        strips_ref[4 * tile : 4 * tile + 4] = strips.reshape(4, SIDE, features)


def gather_rims(received, strips_ref, inner_ref, table_ref, held, corners, row, known):
    near_ref, far_ref, pair_ref, near2_ref, far2_ref = received
    features = strips_ref.shape[-1]
    for strip in range(STRIPS):
        held[strip] = strips_ref[strip]
        corners[strip : strip + 1] = strips_ref[strip, 0:1].astype(F32)
    for slot in range(4):
        held[STRIPS + slot] = pair_ref[slot]
    for slot in range(2):
        held[STRIPS + 4 + slot] = near_ref[slot]
        held[STRIPS + 6 + slot] = far_ref[slot]
    for source, ref in enumerate((pair_ref.at[4], near_ref.at[2], near2_ref.at[2], far_ref.at[2], far2_ref.at[2])):
        corners[(source + 1) * STRIPS : (source + 2) * STRIPS] = ref[...].astype(F32)
    corners[ZERO_ROW : ZERO_ROW + 8] = jnp.zeros((8, features), F32)
    row[...] = jnp.zeros_like(row)
    for tile in range(HERE):
        for side in range(4):
            strip = 4 * tile + side
            known[tile, SIDE * side : SIDE * (side + 1)] = strips_ref[strip]
            known[tile, BORDER + SIDE * side : BORDER + SIDE * (side + 1)] = inner_ref[strip]
            known[tile, 2 * BORDER + SIDE * side : 2 * BORDER + SIDE * (side + 1)] = held[table_ref[strip]]
            row[tile, side : side + 1] = corners[pl.ds(table_ref[STRIPS + strip], 1)]
        known[tile, 3 * BORDER :] = row[tile].astype(BF16)


def border_conv(received, strips_ref, inner_ref, table_ref, weight_ref, border_ref, scratch):
    held, corners, row, known, patches = scratch
    gather_rims(received, strips_ref, inner_ref, table_ref, held, corners, row, known)
    features, width = strips_ref.shape[-1], weight_ref.shape[-1]
    for tile in range(HERE):
        moved = dot(border_ref[...], known[tile]).astype(BF16)
        for tap in range(9):
            patches[tap, BORDER * tile : BORDER * (tile + 1)] = moved[BORDER * tap : BORDER * (tap + 1)]
    for group in range(features // width):
        lanes = slice(width * group, width * (group + 1))
        yield lanes, dot(jnp.concatenate([patches[tap, :, lanes] for tap in range(9)], 1), weight_ref[...])


def border_kernel(last, sends, *refs):
    strips_ref, inner_ref, *received = refs[:7]
    table_ref, weight_ref, border_ref, corners_ref = refs[7:11]
    rest = list(refs[11:])
    state_ref = rest.pop(0) if last else None
    out_ref = rest.pop(0)
    messages = [rest.pop(0) for _ in range(3 if sends else 0)]
    for lanes, total in border_conv(received, strips_ref, inner_ref, table_ref, weight_ref, border_ref, rest):
        if last:
            total = total + state_ref[:, :, lanes].reshape(total.shape).astype(F32)
        else:
            total = gelu(total)
        out_ref[:, :, lanes] = total.astype(BF16).reshape(STRIPS, SIDE, -1)
    if sends:
        address(out_ref, table_ref.at[pl.ds(2 * STRIPS, 8)], *messages, corners_ref)


def tile_conv(field_ref, top, strips_ref, weight_ref, tile_ref, shifted, tile):
    features, width = field_ref.shape[-1], weight_ref.shape[-1]
    strips = strips_ref[4 * tile : 4 * tile + 4].reshape(BORDER, features)
    half, rows = SIDE // 2, INNER // 2
    for group in range(2):
        inner = field_ref[tile, top + rows * group : top + rows * (group + 1)].reshape(rows * SIDE, features)
        moved = dot(tile_ref[group], jnp.concatenate([inner, strips], 0)).astype(BF16)
        shifted[:, half * group : half * (group + 1)] = moved.reshape(3, half, SIDE, features)
    for group in range(features // width):
        lanes = slice(width * group, width * (group + 1))
        windows = [shifted[b, a : a + INNER, :, lanes].reshape(INNER * SIDE, width) for a in range(3) for b in range(3)]
        yield lanes, dot(jnp.concatenate(windows, 1), weight_ref[...])


def inner_kernel(last, top, field_ref, strips_ref, weight_ref, tile_ref, other_ref, out_ref, *rest):
    shifted = rest[-1]
    for tile in range(HERE):
        for lanes, total in tile_conv(field_ref, top, strips_ref, weight_ref, tile_ref, shifted.at[tile], tile):
            if last:
                total = total + other_ref[tile, 1 : 1 + INNER, :, lanes].reshape(total.shape).astype(F32)
            else:
                total = gelu(total)
            out_ref[tile, :, :, lanes] = total.astype(BF16).reshape(INNER, SIDE, -1)
    if not last:
        inner_strips(out_ref, 0, other_ref, rest[0])


def mixer(block, level, mix_in_ref, mix_out_ref, outs):
    levels = mix_in_ref.shape[1] // 128
    order = [level ^ back for back in range(levels)]
    first = jnp.concatenate([mix_in_ref[block, pl.ds(pl.multiple_of(128 * place, 128), 128), :] for place in order], 0)
    second = [mix_out_ref[block, :, pl.ds(pl.multiple_of(128 * place, 128), 128)] for place in order[:outs]]
    second = jnp.concatenate(second, 1) if outs > 1 else second[0]

    def mix(column):
        hidden = gelu(dot(column, first)).astype(BF16)
        return (column[:, : 128 * outs].astype(F32) + dot(hidden, second)).astype(BF16)

    return mix


def mix_strips_kernel(block, own_ref, one_ref, two_ref, three_ref, mix_in_ref, mix_out_ref, table_ref, corners_ref, strips_ref, near_ref, far_ref, pair_ref):
    mix = mixer(block, lax.axis_index("level"), mix_in_ref, mix_out_ref, 4)
    column = jnp.concatenate([ref[...].reshape(STRIPS * SIDE, 128) for ref in (own_ref, one_ref, two_ref, three_ref)], 1)
    strips_ref[...] = mix(column).reshape(STRIPS, SIDE, 512)
    address(strips_ref, table_ref.at[pl.ds(2 * STRIPS, 8)], near_ref, far_ref, pair_ref, corners_ref)


def mix_tiles_kernel(block, own_ref, one_ref, two_ref, three_ref, mix_in_ref, mix_out_ref, inner_ref, out_ref, strips_ref):
    mix = mixer(block, lax.axis_index("level"), mix_in_ref, mix_out_ref, 4)
    for tile in range(HERE):
        column = jnp.concatenate([ref[tile].reshape(INNER * SIDE, 128) for ref in (own_ref, one_ref, two_ref, three_ref)], 1)
        out_ref[tile] = mix(column).reshape(INNER, SIDE, 512)
    inner_strips(out_ref, 0, inner_ref, strips_ref)


def last_inner_kernel(block, field_ref, strips_ref, weight_ref, tile_ref, state_ref, mix_in_ref, mix_out_ref, out_ref, shifted):
    mix = mixer(block, lax.axis_index("level"), mix_in_ref, mix_out_ref, 1)
    for tile in range(HERE):
        columns = []
        for lanes, total in tile_conv(field_ref, 0, strips_ref, weight_ref, tile_ref, shifted.at[tile], tile):
            columns.append((total + state_ref[tile, :, :, lanes].reshape(total.shape).astype(F32)).astype(BF16))
        out_ref[tile] = mix(jnp.concatenate(columns, 1)).reshape(INNER, SIDE, 128)


def last_border_kernel(block, *refs):
    strips_ref, inner_ref, *received = refs[:7]
    table_ref, weight_ref, border_ref, state_ref, mix_in_ref, mix_out_ref, tiles_ref, tile_ref, out_ref = refs[7:16]
    mix = mixer(block, lax.axis_index("level"), mix_in_ref, mix_out_ref, 1)
    columns = []
    for lanes, total in border_conv(received, strips_ref, inner_ref, table_ref, weight_ref, border_ref, refs[16:]):
        columns.append((total + state_ref[:, :, lanes].reshape(total.shape).astype(F32)).astype(BF16))
    mixed = mix(jnp.concatenate(columns, 1))
    half, rows = SIDE // 2, INNER // 2
    for tile in range(HERE):
        strips = mixed[BORDER * tile : BORDER * (tile + 1)]
        for group in range(2):
            inner = tiles_ref[tile, rows * group : rows * (group + 1)].reshape(rows * SIDE, 128)
            place = tile_ref[group, half * SIDE : 2 * half * SIDE]
            merged = dot(place, jnp.concatenate([inner, strips], 0)).astype(BF16)
            out_ref[tile, half * group : half * (group + 1)] = merged.reshape(half, SIDE, 128)


V = pl.BlockSpec(memory_space=pltpu.VMEM)
S = pl.BlockSpec(memory_space=pltpu.SMEM)
H = pl.BlockSpec(memory_space=pltpu.HBM)


def call(kernel, name, in_specs, out_specs, out_shape, scratch, args):
    return pl.pallas_call(
        kernel,
        name=name,
        in_specs=in_specs,
        out_specs=out_specs,
        out_shape=out_shape,
        scratch_shapes=scratch,
        compiler_params=pltpu.CompilerParams(vmem_limit_bytes=VMEM_LIMIT),
    )(*(pltpu.with_memory_space_constraint(arg, pltpu.HBM) if spec is H else arg for spec, arg in zip(in_specs, args)))


def arrays(*shapes):
    return [jax.ShapeDtypeStruct(shape, BF16) for shape in shapes]


def strip_shape(features):
    return STRIPS, SIDE, features


def message_shapes(features):
    return (3, SIDE, features), (3, SIDE, features), (5, SIDE, features)


def border_scratch(features):
    return [
        pltpu.VMEM((STRIPS + 8, SIDE, features), BF16),
        pltpu.VMEM((ZERO_ROW + 8, features), F32),
        pltpu.VMEM((HERE, SIDE, features), F32),
        pltpu.VMEM((HERE, 3 * BORDER + SIDE, features), BF16),
        pltpu.VMEM((9, STRIPS * SIDE, features), BF16),
    ]


def tile_scratch(features):
    return [pltpu.VMEM((HERE, 3, SIDE, SIDE, features), BF16)]


def send(near, far, to_pair):
    faces = lax.axis_size("face")
    apart = [(i, (i + 2) % faces if i & 2 else (i - 2) % faces) for i in range(faces)]
    from_far = lax.ppermute(far, "face", apart)
    from_near = lax.ppermute(near, "face", [(i, i ^ 2) for i in range(faces)])
    return from_near, from_far, lax.ppermute(to_pair, "face", [(i, i ^ 1) for i in range(faces)])


def receive(sent, *beside):
    near, far, paired = sent
    near, far, *beside = lax.optimization_barrier((near, far, *beside))
    pairs = [(i, i ^ 1) for i in range(lax.axis_size("face"))]
    arrived = near, far, paired, lax.ppermute(near, "face", pairs), lax.ppermute(far, "face", pairs)
    return arrived, *beside


def from_level(shard, distance):
    levels = lax.axis_size("level")
    return lax.ppermute(shard, "level", [(i, i ^ distance) for i in range(levels)])


def shards(state, conv_weight, mix_in, mix_out, edge_source, corner_source):
    faces = lax.axis_size("face")
    thin = state.shape[-1]
    wide = 4 * thin
    border_hbm, tile_hbm, inner_hbm = (jnp.asarray(t) for t in (border_table(), tile_table(), inner_table()))
    edges, cornered = edge_source.T, corner_source.T
    edge_scratch = pltpu.SMEM(edges.shape, I32)

    strips, *messages, sends, state, corners = call(
        functools.partial(first_kernel, faces), "first",
        [H, H], [V, V, V, V, S, V, V],
        arrays(strip_shape(thin), *message_shapes(thin))
        + [jax.ShapeDtypeStruct((8,), I32)]
        + arrays(state.shape, (STRIPS, STRIPS * SIDE)),
        [edge_scratch, pltpu.SMEM((16,), I32), pltpu.SemaphoreType.DMA((2,))],
        (state, edges),
    )
    sent = send(*messages)
    table, narrow1, narrow2, borders, tiled, inner_places, state_inner = call(
        functools.partial(side_kernel, faces), "side",
        [H] * 6 + [S, V], [S] + [V] * 6,
        [jax.ShapeDtypeStruct((2 * STRIPS + 8,), I32)]
        + arrays((1152, 128), (1152, 128), border_hbm.shape, tile_hbm.shape, inner_hbm.shape, strip_shape(thin)),
        [edge_scratch, edge_scratch, pltpu.VMEM(conv_weight.shape[1:], BF16), pltpu.SemaphoreType.DMA((6,))],
        (edges, cornered, conv_weight, border_hbm, tile_hbm, inner_hbm, sends, state),
    )

    def border(last, sending, strips, inner_strips, received, weight, residual=()):
        size = strips.shape[-1]
        shapes = [strip_shape(size), *(message_shapes(size) if sending else ())]
        return call(
            functools.partial(border_kernel, last, sending), f"border_{size}_{int(last)}",
            [V] * 7 + [S] + [V] * 3 + [V] * len(residual), [V] * len(shapes),
            arrays(*shapes), border_scratch(size),
            (strips, inner_strips, *received, table, weight, borders, corners, *residual),
        )

    def interior(last, top, field, strips, weight, other):
        size = field.shape[-1]
        shapes = [(HERE, INNER, SIDE, size)] + ([] if last else [strip_shape(size)])
        return call(
            functools.partial(inner_kernel, last, top), f"inner_{size}_{int(last)}",
            [V] * 5, [V] * len(shapes), arrays(*shapes), tile_scratch(size),
            (field, strips, weight, tiled, other),
        )

    inner, inner_ring = interior(False, 1, state, strips, narrow1, inner_places)
    received, inner, inner_ring = receive(sent, inner, inner_ring)
    inner_edge, *messages = border(False, True, strips, state_inner, received, narrow1)

    sent = send(*messages)
    (field,) = interior(True, 0, inner, inner_edge, narrow2, state)
    one, three = from_level(field, 1), from_level(field, 3)
    received, _ = receive(sent, field)
    (edge,) = border(True, False, inner_edge, inner_ring, received, narrow2, (strips,))

    narrow3, narrow4, wide1, wide2, mix_in, mix_out = call(
        weights_kernel, "weights", [H] * 3 + [V], [V] * 6,
        arrays((1152, 128), (1152, 128), (2304, 256), (2304, 256), mix_in.shape, mix_out.shape),
        [pltpu.VMEM(conv_weight.shape[1:], BF16), pltpu.SemaphoreType.DMA((3,))],
        (conv_weight, mix_in, mix_out, edge),
    )
    three, edge = lax.optimization_barrier((three, edge))
    fields = [field, one, from_level(three, 1), three]
    edge_parts = [edge] + [from_level(edge, d) for d in (1, 2, 3)]
    strips, *messages = call(
        functools.partial(mix_strips_kernel, 0), "mix_strips",
        [V] * 6 + [S, V], [V] * 4,
        arrays(strip_shape(wide), *message_shapes(wide)), [],
        (*edge_parts, mix_in, mix_out, table, corners),
    )
    sent = send(*messages)
    field, ring1 = call(
        functools.partial(mix_tiles_kernel, 0), "mix_tiles",
        [V] * 7, [V] * 2, arrays((HERE, INNER, SIDE, wide), strip_shape(wide)), [],
        (*fields, mix_in, mix_out, inner_places),
    )
    inner, inner_ring = interior(False, 0, field, strips, wide1, inner_places)
    received, inner, inner_ring = receive(sent, inner, inner_ring)
    inner_edge, *messages = border(False, True, strips, ring1, received, narrow3)

    sent = send(*messages)
    tiles = call(
        functools.partial(last_inner_kernel, 1), "last_inner",
        [V] * 7, V, arrays((HERE, INNER, SIDE, thin))[0], tile_scratch(wide),
        (inner, inner_edge, wide2, tiled, field, mix_in, mix_out),
    )
    received, tiles = receive(sent, tiles)
    return call(
        functools.partial(last_border_kernel, 1), "last_border",
        [V] * 7 + [S] + [V] * 7, V, arrays((HERE, SIDE, SIDE, thin))[0], border_scratch(wide),
        (inner_edge, inner_ring, *received, table, narrow4, borders, strips, mix_in, mix_out, tiles, tiled),
    )


def solution(mesh):
    return jax.shard_map(
        shards,
        mesh=mesh,
        in_specs=(P(("ens", "face"), None, None, "level"), P(), P(), P(), P(), P()),
        out_specs=P(("ens", "face"), None, None, "level"),
        check_vma=False,
    )
```

```python
import functools

import jax
import jax.numpy as jnp
import numpy as np
from jax import lax
from jax.experimental import pallas as pl
from jax.experimental.pallas import tpu as pltpu
from jax.sharding import PartitionSpec as P

BF16, F32, I32 = jnp.bfloat16, jnp.float32, jnp.int32
SIDE = 16
INNER = SIDE - 2
PIXELS = SIDE * SIDE
HERE = 4
STRIPS = 4 * HERE
BORDER = 4 * SIDE
ZERO_ROW = 6 * STRIPS
VMEM_LIMIT = 16 * 1024 * 1024


def one_hot(columns, width):
    table = np.zeros((len(columns), width), np.float32)
    for row, column in enumerate(columns):
        if column is not None:
            table[row, column] = 1.0
    return table.astype(jnp.bfloat16)


def strip_pixel(side, k, depth=0):
    last = SIDE - 1
    return ((depth, k), (k, last - depth), (last - depth, last - k), (last - k, depth))[side]


def ring(depth):
    places = {}
    for side in range(4):
        for k in range(depth, SIDE - depth):
            places.setdefault(strip_pixel(side, k, depth), SIDE * side + k)
    return places


def border_table():
    outer, inner, last = ring(0), ring(1), SIDE - 1
    corner = {(-1, -1): 0, (-1, SIDE): 1, (SIDE, SIDE): 2, (SIDE, -1): 3}
    columns = []
    for a in range(3):
        for b in range(3):
            for side in range(4):
                for k in range(SIDE):
                    i, j = strip_pixel(side, k)
                    i, j = i + a - 1, j + b - 1
                    if (i, j) in corner:
                        columns.append(3 * BORDER + corner[i, j])
                    elif i < 0:
                        columns.append(2 * BORDER + last - j)
                    elif j > last:
                        columns.append(2 * BORDER + SIDE + last - i)
                    elif i > last:
                        columns.append(2 * BORDER + 2 * SIDE + j)
                    elif j < 0:
                        columns.append(2 * BORDER + 3 * SIDE + i)
                    elif (i, j) in outer:
                        columns.append(outer[i, j])
                    else:
                        columns.append(BORDER + inner[i, j])
    return one_hot(columns, 3 * BORDER + SIDE)


def tile_table():
    outer, half = ring(0), INNER // 2
    groups = []
    for group in range(2):
        columns = []
        for b in range(3):
            for i in range(SIDE // 2 * group, SIDE // 2 * (group + 1)):
                for j in range(SIDE):
                    column = j + b - 1
                    if column < 0 or column >= SIDE:
                        columns.append(None)
                    elif (i, column) in outer:
                        columns.append(half * SIDE + outer[i, column])
                    else:
                        columns.append((i - 1 - half * group) * SIDE + column)
        groups.append(one_hot(columns, half * SIDE + BORDER))
    return np.stack(groups)


def inner_table():
    columns = []
    for side in range(4):
        for k in range(SIDE):
            i, j = strip_pixel(side, k, 1)
            columns.append((i - 1) * SIDE + j if 1 <= k < SIDE - 1 else None)
    return one_hot(columns, INNER * SIDE)


def dot(a, b):
    return jnp.dot(a, b, preferred_element_type=F32)


def gelu(z):
    return z * (0.5 + 0.5 * jnp.tanh(z * (0.7978845608028654 + 0.035677408136300125 * (z * z))))


def copies(sems, *pairs):
    started = [pltpu.make_async_copy(source, target, sems.at[n]) for n, (source, target) in enumerate(pairs)]
    for copy in started:
        copy.start()
    return started


def address(strips_ref, send_ref, near_ref, far_ref, pair_ref, corners_ref):
    features = strips_ref.shape[-1]
    corners = dot(corners_ref[...], strips_ref[...].reshape(STRIPS * SIDE, features)).astype(BF16)
    for slot in range(4):
        pair_ref[slot] = strips_ref[send_ref[slot]]
    for slot in range(2):
        near_ref[slot] = strips_ref[send_ref[4 + slot]]
        far_ref[slot] = strips_ref[send_ref[6 + slot]]
    pair_ref[4] = corners
    near_ref[2] = corners
    far_ref[2] = corners


def neighbours(faces):
    own = lax.axis_index("face")
    ahead, behind = lax.rem(own + 2, faces), lax.rem(own + faces - 2, faces)
    return own, own ^ 1, own ^ 2, jnp.where(own & 2 == 0, behind, ahead)


def first_kernel(faces, state_ref, edge_ref, strips_ref, near_ref, far_ref, pair_ref, table_ref, held_ref, corners_ref, edges, send, sems):
    edge_copy, state_copy = copies(sems, (edge_ref, edges), (state_ref, held_ref))
    row = lax.broadcasted_iota(I32, (BORDER, PIXELS), 0)
    column = lax.broadcasted_iota(I32, (BORDER, PIXELS), 1)
    side, k, last = row // SIDE, row % SIDE, SIDE - 1
    place = jnp.where(
        side == 0,
        k,
        jnp.where(side == 1, k * SIDE + last, jnp.where(side == 2, last * SIDE + last - k, (last - k) * SIDE)),
    )
    picks = (place == column).astype(F32).astype(BF16)
    row = lax.broadcasted_iota(I32, (STRIPS, STRIPS * SIDE), 0)
    column = lax.broadcasted_iota(I32, (STRIPS, STRIPS * SIDE), 1)
    corners_ref[...] = (row * SIDE == column).astype(F32).astype(BF16)
    own, paired, near, far = neighbours(faces)
    edge_copy.wait()
    for target, start, capacity in ((paired, 0, 4), (near, 4, 2), (far, 6, 2)):
        taken = jnp.int32(0)
        for strip in range(STRIPS):
            wanted = edges[strip % 4, target * HERE + strip // 4]
            fits = jnp.logical_and(wanted >> 4 == own, taken < capacity)
            send[jnp.where(fits, start + taken, 8)] = wanted & 15
            taken = taken + fits.astype(I32)
    for slot in range(8):
        table_ref[slot] = send[slot]
    state_copy.wait()
    features = state_ref.shape[-1]
    for tile in range(HERE):
        strips = dot(picks, held_ref[tile].reshape(PIXELS, features)).astype(BF16)
        strips_ref[4 * tile : 4 * tile + 4] = strips.reshape(4, SIDE, features)
    address(strips_ref, send, near_ref, far_ref, pair_ref, corners_ref)


def side_kernel(faces, *refs):
    edge_ref, corner_ref, conv_ref, border_ref, tile_ref, inner_ref, send_ref, state_ref = refs[:8]
    table_ref, narrow1_ref, narrow2_ref, border_held, tile_held, inner_held, strips_ref = refs[8:15]
    edges, cornered, conv, sems = refs[15:]
    started = copies(
        sems,
        (edge_ref, edges),
        (corner_ref, cornered),
        (conv_ref.at[0], conv),
        (inner_ref, inner_held),
        (border_ref, border_held),
        (tile_ref, tile_held),
    )
    for narrow in (narrow1_ref, narrow2_ref):
        narrow[...] = jnp.zeros_like(narrow)
    own, paired, near, far = neighbours(faces)
    from_pair, from_near, from_far = jnp.int32(0), jnp.int32(0), jnp.int32(0)
    for copy in started[:4]:
        copy.wait()
    for slot in range(8):
        table_ref[2 * STRIPS + slot] = send_ref[slot]
    for strip in range(STRIPS):
        wanted = edges[strip % 4, own * HERE + strip // 4]
        holder, place = wanted >> 4, wanted & 15
        by_pair, by_near, mine = holder == paired, holder == near, holder == own
        by_far = jnp.logical_not(mine | by_pair | by_near)
        table_ref[strip] = jnp.where(
            mine,
            place,
            jnp.where(
                by_pair,
                STRIPS + jnp.minimum(from_pair, 3),
                jnp.where(
                    by_near,
                    STRIPS + 4 + jnp.minimum(from_near, 1),
                    STRIPS + 6 + jnp.minimum(from_far, 1),
                ),
            ),
        )
        from_pair = from_pair + by_pair.astype(I32)
        from_near = from_near + by_near.astype(I32)
        from_far = from_far + by_far.astype(I32)
    for corner in range(STRIPS):
        wanted = cornered[corner % 4, own * HERE + corner // 4]
        safe = jnp.maximum(wanted, 0)
        holder, place = safe >> 4, safe & 15
        source = jnp.where(
            holder == own,
            0,
            jnp.where(
                holder == paired,
                1,
                jnp.where(holder == near, 2, jnp.where(holder == (near ^ 1), 3, jnp.where(holder == far, 4, 5))),
            ),
        )
        table_ref[STRIPS + corner] = jnp.where(wanted < 0, ZERO_ROW, source * STRIPS + place)
    for layer, narrow in enumerate((narrow1_ref, narrow2_ref)):
        spread(conv, layer, narrow)
    inner_strips(state_ref, 1, inner_held, strips_ref)
    for copy in started[4:]:
        copy.wait()


def spread(conv, layer, weight):
    width = weight.shape[-1]
    for tap in range(9):
        for level in range(width // 64):
            weight[pl.ds(width * tap + 64 * level, 64), pl.ds(64 * level, 64)] = conv[layer, tap]


def weights_kernel(*refs):
    conv_ref, mix_in_ref, mix_out_ref, _, narrow1_ref, narrow2_ref, wide1_ref, wide2_ref, mix_in_held, mix_out_held, conv, sems = refs
    started = copies(sems, (conv_ref.at[1], conv), (mix_in_ref, mix_in_held), (mix_out_ref, mix_out_held))
    for weight in (narrow1_ref, narrow2_ref, wide1_ref, wide2_ref):
        weight[...] = jnp.zeros_like(weight)
    started[0].wait()
    for layer, weights in enumerate(((narrow1_ref, wide1_ref), (narrow2_ref, wide2_ref))):
        for weight in weights:
            spread(conv, layer, weight)
    for copy in started[1:]:
        copy.wait()


def inner_strips(field_ref, top, inner_ref, strips_ref):
    features = field_ref.shape[-1]
    for tile in range(HERE):
        rows = field_ref[tile, top : top + INNER].reshape(INNER * SIDE, features)
        strips = dot(inner_ref[...], rows).astype(BF16)
        strips_ref[4 * tile : 4 * tile + 4] = strips.reshape(4, SIDE, features)


def gather_rims(received, strips_ref, inner_ref, table_ref, held, corners, row, known):
    near_ref, far_ref, pair_ref, near2_ref, far2_ref = received
    features = strips_ref.shape[-1]
    for strip in range(STRIPS):
        held[strip] = strips_ref[strip]
        corners[strip : strip + 1] = strips_ref[strip, 0:1].astype(F32)
    for slot in range(4):
        held[STRIPS + slot] = pair_ref[slot]
    for slot in range(2):
        held[STRIPS + 4 + slot] = near_ref[slot]
        held[STRIPS + 6 + slot] = far_ref[slot]
    for source, ref in enumerate((pair_ref.at[4], near_ref.at[2], near2_ref.at[2], far_ref.at[2], far2_ref.at[2])):
        corners[(source + 1) * STRIPS : (source + 2) * STRIPS] = ref[...].astype(F32)
    corners[ZERO_ROW : ZERO_ROW + 8] = jnp.zeros((8, features), F32)
    row[...] = jnp.zeros_like(row)
    for tile in range(HERE):
        for side in range(4):
            strip = 4 * tile + side
            known[tile, SIDE * side : SIDE * (side + 1)] = strips_ref[strip]
            known[tile, BORDER + SIDE * side : BORDER + SIDE * (side + 1)] = inner_ref[strip]
            known[tile, 2 * BORDER + SIDE * side : 2 * BORDER + SIDE * (side + 1)] = held[table_ref[strip]]
            row[tile, side : side + 1] = corners[pl.ds(table_ref[STRIPS + strip], 1)]
        known[tile, 3 * BORDER :] = row[tile].astype(BF16)


def border_conv(received, strips_ref, inner_ref, table_ref, weight_ref, border_ref, scratch):
    held, corners, row, known, patches = scratch
    gather_rims(received, strips_ref, inner_ref, table_ref, held, corners, row, known)
    features, width = strips_ref.shape[-1], weight_ref.shape[-1]
    for tile in range(HERE):
        moved = dot(border_ref[...], known[tile]).astype(BF16)
        for tap in range(9):
            patches[tap, BORDER * tile : BORDER * (tile + 1)] = moved[BORDER * tap : BORDER * (tap + 1)]
    for group in range(features // width):
        lanes = slice(width * group, width * (group + 1))
        yield lanes, dot(jnp.concatenate([patches[tap, :, lanes] for tap in range(9)], 1), weight_ref[...])


def border_kernel(last, sends, *refs):
    strips_ref, inner_ref, *received = refs[:7]
    table_ref, weight_ref, border_ref, corners_ref = refs[7:11]
    rest = list(refs[11:])
    state_ref = rest.pop(0) if last else None
    out_ref = rest.pop(0)
    messages = [rest.pop(0) for _ in range(3 if sends else 0)]
    for lanes, total in border_conv(received, strips_ref, inner_ref, table_ref, weight_ref, border_ref, rest):
        if last:
            total = total + state_ref[:, :, lanes].reshape(total.shape).astype(F32)
        else:
            total = gelu(total)
        out_ref[:, :, lanes] = total.astype(BF16).reshape(STRIPS, SIDE, -1)
    if sends:
        address(out_ref, table_ref.at[pl.ds(2 * STRIPS, 8)], *messages, corners_ref)


def tile_conv(field_ref, top, strips_ref, weight_ref, tile_ref, shifted, tile):
    features, width = field_ref.shape[-1], weight_ref.shape[-1]
    strips = strips_ref[4 * tile : 4 * tile + 4].reshape(BORDER, features)
    half, rows = SIDE // 2, INNER // 2
    for group in range(2):
        inner = field_ref[tile, top + rows * group : top + rows * (group + 1)].reshape(rows * SIDE, features)
        moved = dot(tile_ref[group], jnp.concatenate([inner, strips], 0)).astype(BF16)
        shifted[:, half * group : half * (group + 1)] = moved.reshape(3, half, SIDE, features)
    for group in range(features // width):
        lanes = slice(width * group, width * (group + 1))
        windows = [shifted[b, a : a + INNER, :, lanes].reshape(INNER * SIDE, width) for a in range(3) for b in range(3)]
        yield lanes, dot(jnp.concatenate(windows, 1), weight_ref[...])


def inner_kernel(last, top, field_ref, strips_ref, weight_ref, tile_ref, other_ref, out_ref, *rest):
    shifted = rest[-1]
    for tile in range(HERE):
        for lanes, total in tile_conv(field_ref, top, strips_ref, weight_ref, tile_ref, shifted.at[tile], tile):
            if last:
                total = total + other_ref[tile, 1 : 1 + INNER, :, lanes].reshape(total.shape).astype(F32)
            else:
                total = gelu(total)
            out_ref[tile, :, :, lanes] = total.astype(BF16).reshape(INNER, SIDE, -1)
    if not last:
        inner_strips(out_ref, 0, other_ref, rest[0])


def mixer(block, level, mix_in_ref, mix_out_ref, outs):
    levels = mix_in_ref.shape[1] // 128
    order = [level ^ back for back in range(levels)]
    first = jnp.concatenate([mix_in_ref[block, pl.ds(pl.multiple_of(128 * place, 128), 128), :] for place in order], 0)
    second = [mix_out_ref[block, :, pl.ds(pl.multiple_of(128 * place, 128), 128)] for place in order[:outs]]
    second = jnp.concatenate(second, 1) if outs > 1 else second[0]

    def mix(column):
        hidden = gelu(dot(column, first)).astype(BF16)
        return (column[:, : 128 * outs].astype(F32) + dot(hidden, second)).astype(BF16)

    return mix


def mix_strips_kernel(block, own_ref, one_ref, two_ref, three_ref, mix_in_ref, mix_out_ref, table_ref, corners_ref, strips_ref, near_ref, far_ref, pair_ref):
    mix = mixer(block, lax.axis_index("level"), mix_in_ref, mix_out_ref, 4)
    column = jnp.concatenate([ref[...].reshape(STRIPS * SIDE, 128) for ref in (own_ref, one_ref, two_ref, three_ref)], 1)
    strips_ref[...] = mix(column).reshape(STRIPS, SIDE, 512)
    address(strips_ref, table_ref.at[pl.ds(2 * STRIPS, 8)], near_ref, far_ref, pair_ref, corners_ref)


def mix_tiles_kernel(block, own_ref, one_ref, two_ref, three_ref, mix_in_ref, mix_out_ref, inner_ref, out_ref, strips_ref):
    mix = mixer(block, lax.axis_index("level"), mix_in_ref, mix_out_ref, 4)
    for tile in range(HERE):
        column = jnp.concatenate([ref[tile].reshape(INNER * SIDE, 128) for ref in (own_ref, one_ref, two_ref, three_ref)], 1)
        out_ref[tile] = mix(column).reshape(INNER, SIDE, 512)
    inner_strips(out_ref, 0, inner_ref, strips_ref)


def last_inner_kernel(block, field_ref, strips_ref, weight_ref, tile_ref, state_ref, mix_in_ref, mix_out_ref, out_ref, shifted):
    mix = mixer(block, lax.axis_index("level"), mix_in_ref, mix_out_ref, 1)
    for tile in range(HERE):
        columns = []
        for lanes, total in tile_conv(field_ref, 0, strips_ref, weight_ref, tile_ref, shifted.at[tile], tile):
            columns.append((total + state_ref[tile, :, :, lanes].reshape(total.shape).astype(F32)).astype(BF16))
        out_ref[tile] = mix(jnp.concatenate(columns, 1)).reshape(INNER, SIDE, 128)


def last_border_kernel(block, *refs):
    strips_ref, inner_ref, *received = refs[:7]
    table_ref, weight_ref, border_ref, state_ref, mix_in_ref, mix_out_ref, tiles_ref, tile_ref, out_ref = refs[7:16]
    mix = mixer(block, lax.axis_index("level"), mix_in_ref, mix_out_ref, 1)
    columns = []
    for lanes, total in border_conv(received, strips_ref, inner_ref, table_ref, weight_ref, border_ref, refs[16:]):
        columns.append((total + state_ref[:, :, lanes].reshape(total.shape).astype(F32)).astype(BF16))
    mixed = mix(jnp.concatenate(columns, 1))
    half, rows = SIDE // 2, INNER // 2
    for tile in range(HERE):
        strips = mixed[BORDER * tile : BORDER * (tile + 1)]
        for group in range(2):
            inner = tiles_ref[tile, rows * group : rows * (group + 1)].reshape(rows * SIDE, 128)
            place = tile_ref[group, half * SIDE : 2 * half * SIDE]
            merged = dot(place, jnp.concatenate([inner, strips], 0)).astype(BF16)
            out_ref[tile, half * group : half * (group + 1)] = merged.reshape(half, SIDE, 128)


V = pl.BlockSpec(memory_space=pltpu.VMEM)
S = pl.BlockSpec(memory_space=pltpu.SMEM)
H = pl.BlockSpec(memory_space=pltpu.HBM)


def call(kernel, name, in_specs, out_specs, out_shape, scratch, args):
    return pl.pallas_call(
        kernel,
        name=name,
        in_specs=in_specs,
        out_specs=out_specs,
        out_shape=out_shape,
        scratch_shapes=scratch,
        compiler_params=pltpu.CompilerParams(vmem_limit_bytes=VMEM_LIMIT),
    )(*(pltpu.with_memory_space_constraint(arg, pltpu.HBM) if spec is H else arg for spec, arg in zip(in_specs, args)))


def arrays(*shapes):
    return [jax.ShapeDtypeStruct(shape, BF16) for shape in shapes]


def strip_shape(features):
    return STRIPS, SIDE, features


def message_shapes(features):
    return (3, SIDE, features), (3, SIDE, features), (5, SIDE, features)


def border_scratch(features):
    return [
        pltpu.VMEM((STRIPS + 8, SIDE, features), BF16),
        pltpu.VMEM((ZERO_ROW + 8, features), F32),
        pltpu.VMEM((HERE, SIDE, features), F32),
        pltpu.VMEM((HERE, 3 * BORDER + SIDE, features), BF16),
        pltpu.VMEM((9, STRIPS * SIDE, features), BF16),
    ]


def tile_scratch(features):
    return [pltpu.VMEM((HERE, 3, SIDE, SIDE, features), BF16)]


def send(near, far, to_pair):
    faces = lax.axis_size("face")
    apart = [(i, (i + 2) % faces if i & 2 else (i - 2) % faces) for i in range(faces)]
    from_far = lax.ppermute(far, "face", apart)
    from_near = lax.ppermute(near, "face", [(i, i ^ 2) for i in range(faces)])
    return from_near, from_far, lax.ppermute(to_pair, "face", [(i, i ^ 1) for i in range(faces)])


def receive(sent, *beside):
    near, far, paired = sent
    near, far, *beside = lax.optimization_barrier((near, far, *beside))
    pairs = [(i, i ^ 1) for i in range(lax.axis_size("face"))]
    arrived = near, far, paired, lax.ppermute(near, "face", pairs), lax.ppermute(far, "face", pairs)
    return arrived, *beside


def from_level(shard, distance):
    levels = lax.axis_size("level")
    return lax.ppermute(shard, "level", [(i, i ^ distance) for i in range(levels)])


def shards(state, conv_weight, mix_in, mix_out, edge_source, corner_source):
    faces = lax.axis_size("face")
    thin = state.shape[-1]
    wide = 4 * thin
    border_hbm, tile_hbm, inner_hbm = (jnp.asarray(t) for t in (border_table(), tile_table(), inner_table()))
    edges, cornered = edge_source.T, corner_source.T
    edge_scratch = pltpu.SMEM(edges.shape, I32)

    strips, *messages, sends, state, corners = call(
        functools.partial(first_kernel, faces), "first",
        [H, H], [V, V, V, V, S, V, V],
        arrays(strip_shape(thin), *message_shapes(thin))
        + [jax.ShapeDtypeStruct((8,), I32)]
        + arrays(state.shape, (STRIPS, STRIPS * SIDE)),
        [edge_scratch, pltpu.SMEM((16,), I32), pltpu.SemaphoreType.DMA((2,))],
        (state, edges),
    )
    sent = send(*messages)
    table, narrow1, narrow2, borders, tiled, inner_places, state_inner = call(
        functools.partial(side_kernel, faces), "side",
        [H] * 6 + [S, V], [S] + [V] * 6,
        [jax.ShapeDtypeStruct((2 * STRIPS + 8,), I32)]
        + arrays((1152, 128), (1152, 128), border_hbm.shape, tile_hbm.shape, inner_hbm.shape, strip_shape(thin)),
        [edge_scratch, edge_scratch, pltpu.VMEM(conv_weight.shape[1:], BF16), pltpu.SemaphoreType.DMA((6,))],
        (edges, cornered, conv_weight, border_hbm, tile_hbm, inner_hbm, sends, state),
    )

    def border(last, sending, strips, inner_strips, received, weight, residual=()):
        size = strips.shape[-1]
        shapes = [strip_shape(size), *(message_shapes(size) if sending else ())]
        return call(
            functools.partial(border_kernel, last, sending), f"border_{size}_{int(last)}",
            [V] * 7 + [S] + [V] * 3 + [V] * len(residual), [V] * len(shapes),
            arrays(*shapes), border_scratch(size),
            (strips, inner_strips, *received, table, weight, borders, corners, *residual),
        )

    def interior(last, top, field, strips, weight, other):
        size = field.shape[-1]
        shapes = [(HERE, INNER, SIDE, size)] + ([] if last else [strip_shape(size)])
        return call(
            functools.partial(inner_kernel, last, top), f"inner_{size}_{int(last)}",
            [V] * 5, [V] * len(shapes), arrays(*shapes), tile_scratch(size),
            (field, strips, weight, tiled, other),
        )

    received, table = receive(sent, table)
    inner_edge, *messages = border(False, True, strips, state_inner, received, narrow1)

    sent = send(*messages)
    inner, inner_ring = interior(False, 1, state, strips, narrow1, inner_places)
    (field,) = interior(True, 0, inner, inner_edge, narrow2, state)
    received, inner_ring, field = receive(sent, inner_ring, field)
    *received, field = lax.optimization_barrier((*received, field))
    one, three = from_level(field, 1), from_level(field, 3)
    (edge,) = border(True, False, inner_edge, inner_ring, received, narrow2, (strips,))

    parts = [from_level(edge, d) for d in (2, 1, 3)]
    narrow3, narrow4, wide1, wide2, mix_in, mix_out = call(
        weights_kernel, "weights", [H] * 3 + [V], [V] * 6,
        arrays((1152, 128), (1152, 128), (2304, 256), (2304, 256), mix_in.shape, mix_out.shape),
        [pltpu.VMEM(conv_weight.shape[1:], BF16), pltpu.SemaphoreType.DMA((3,))],
        (conv_weight, mix_in, mix_out, edge),
    )
    *parts, mix_in, three = lax.optimization_barrier((*parts, mix_in, three))
    edge_parts = [edge, parts[1], parts[0], parts[2]]
    fields = [field, one, from_level(three, 1), three]
    strips, *messages = call(
        functools.partial(mix_strips_kernel, 0), "mix_strips",
        [V] * 6 + [S, V], [V] * 4,
        arrays(strip_shape(wide), *message_shapes(wide)), [],
        (*edge_parts, mix_in, mix_out, table, corners),
    )
    sent = send(*messages)
    field, ring1 = call(
        functools.partial(mix_tiles_kernel, 0), "mix_tiles",
        [V] * 7, [V] * 2, arrays((HERE, INNER, SIDE, wide), strip_shape(wide)), [],
        (*fields, mix_in, mix_out, inner_places),
    )
    received, ring1 = receive(sent, ring1)
    inner_edge, *messages = border(False, True, strips, ring1, received, narrow3)

    sent = send(*messages)
    inner, inner_ring = interior(False, 0, field, strips, wide1, inner_places)
    tiles = call(
        functools.partial(last_inner_kernel, 1), "last_inner",
        [V] * 7, V, arrays((HERE, INNER, SIDE, thin))[0], tile_scratch(wide),
        (inner, inner_edge, wide2, tiled, field, mix_in, mix_out),
    )
    received, tiles, inner_ring = receive(sent, tiles, inner_ring)
    return call(
        functools.partial(last_border_kernel, 1), "last_border",
        [V] * 7 + [S] + [V] * 7, V, arrays((HERE, SIDE, SIDE, thin))[0], border_scratch(wide),
        (inner_edge, inner_ring, *received, table, narrow4, borders, strips, mix_in, mix_out, tiles, tiled),
    )


def solution(mesh):
    return jax.shard_map(
        shards,
        mesh=mesh,
        in_specs=(P(("ens", "face"), None, None, "level"), P(), P(), P(), P(), P()),
        out_specs=P(("ens", "face"), None, None, "level"),
        check_vma=False,
    )
```

```python
import functools

import jax
import jax.numpy as jnp
import numpy as np
from jax import lax
from jax.experimental import pallas as pl
from jax.experimental.pallas import tpu as pltpu
from jax.sharding import PartitionSpec as P

BF16, F32, I32 = jnp.bfloat16, jnp.float32, jnp.int32
SIDE = 16
INNER = SIDE - 2
PIXELS = SIDE * SIDE
HERE = 4
STRIPS = 4 * HERE
BORDER = 4 * SIDE
ZERO_ROW = 6 * STRIPS
VMEM_LIMIT = 16 * 1024 * 1024


def one_hot(columns, width):
    table = np.zeros((len(columns), width), np.float32)
    for row, column in enumerate(columns):
        if column is not None:
            table[row, column] = 1.0
    return table.astype(jnp.bfloat16)


def strip_pixel(side, k, depth=0):
    last = SIDE - 1
    return ((depth, k), (k, last - depth), (last - depth, last - k), (last - k, depth))[side]


def ring(depth):
    places = {}
    for side in range(4):
        for k in range(depth, SIDE - depth):
            places.setdefault(strip_pixel(side, k, depth), SIDE * side + k)
    return places


def border_table():
    outer, inner, last = ring(0), ring(1), SIDE - 1
    corner = {(-1, -1): 0, (-1, SIDE): 1, (SIDE, SIDE): 2, (SIDE, -1): 3}
    columns = []
    for a in range(3):
        for b in range(3):
            for side in range(4):
                for k in range(SIDE):
                    i, j = strip_pixel(side, k)
                    i, j = i + a - 1, j + b - 1
                    if (i, j) in corner:
                        columns.append(3 * BORDER + corner[i, j])
                    elif i < 0:
                        columns.append(2 * BORDER + last - j)
                    elif j > last:
                        columns.append(2 * BORDER + SIDE + last - i)
                    elif i > last:
                        columns.append(2 * BORDER + 2 * SIDE + j)
                    elif j < 0:
                        columns.append(2 * BORDER + 3 * SIDE + i)
                    elif (i, j) in outer:
                        columns.append(outer[i, j])
                    else:
                        columns.append(BORDER + inner[i, j])
    return one_hot(columns, 3 * BORDER + SIDE)


STARTS = 0, 3, 7, 10


def known_rows(group, paired):
    outer, places = ring(0), {}
    for tile in range(2):
        for (i, j), place in outer.items():
            places[tile, i, j] = 2 * BORDER + BORDER * tile + place
        for row in range(4):
            for j in range(1, SIDE - 1):
                i = STARTS[group] + row + 1
                if 1 <= i < SIDE - 1:
                    apart = BORDER * (j % 2) + SIDE * row + 8 * tile + j // 2
                    places[tile, i, j] = apart if paired else BORDER * tile + SIDE * row + j
    return places


def tile_table(paired):
    groups = []
    for group in range(4):
        places, columns = known_rows(group, paired), []
        for shift in range(4):
            for i in range(4 * group, 4 * group + 4):
                for tile in range(2):
                    columns += [places.get((tile, i, 2 * n + shift - 1)) for n in range(8)]
        groups.append(one_hot(columns, 4 * BORDER))
    return np.stack(groups)


def merge_table():
    groups = []
    for group in range(4):
        places = known_rows(group, True)
        rows = range(4 * group, 4 * group + 4)
        columns = [places[tile, i, j] for tile in range(2) for i in rows for j in range(SIDE)]
        groups.append(one_hot(columns, 4 * BORDER))
    return np.stack(groups)


def inner_table():
    columns = []
    for side in range(4):
        for k in range(SIDE):
            i, j = strip_pixel(side, k, 1)
            columns.append((i - 1) * SIDE + j if 1 <= k < SIDE - 1 else None)
    return one_hot(columns, INNER * SIDE)


def paired_inner_table():
    columns = []
    for tile in range(2):
        for side in range(4):
            for k in range(SIDE):
                i, j = strip_pixel(side, k, 1)
                place = INNER * SIDE * (j % 2) + SIDE * (i - 1) + 8 * tile + j // 2
                columns.append(place if 1 <= k < SIDE - 1 else None)
    return one_hot(columns, 2 * INNER * SIDE)


def dot(a, b):
    return jnp.dot(a, b, preferred_element_type=F32)


def gelu(z):
    return z * (0.5 + 0.5 * jnp.tanh(z * (0.7978845608028654 + 0.035677408136300125 * (z * z))))


def copies(sems, *pairs):
    started = [pltpu.make_async_copy(source, target, sems.at[n]) for n, (source, target) in enumerate(pairs)]
    for copy in started:
        copy.start()
    return started


def address(strips_ref, send_ref, near_ref, far_ref, pair_ref, corners_ref):
    features = strips_ref.shape[-1]
    corners = dot(corners_ref[...], strips_ref[...].reshape(STRIPS * SIDE, features)).astype(BF16)
    for slot in range(4):
        pair_ref[slot] = strips_ref[send_ref[slot]]
    for slot in range(2):
        near_ref[slot] = strips_ref[send_ref[4 + slot]]
        far_ref[slot] = strips_ref[send_ref[6 + slot]]
    pair_ref[4] = corners
    near_ref[2] = corners
    far_ref[2] = corners


def neighbours(faces):
    own = lax.axis_index("face")
    ahead, behind = lax.rem(own + 2, faces), lax.rem(own + faces - 2, faces)
    return own, own ^ 1, own ^ 2, jnp.where(own & 2 == 0, behind, ahead)


def first_kernel(faces, state_ref, edge_ref, strips_ref, near_ref, far_ref, pair_ref, table_ref, held_ref, corners_ref, edges, send, sems):
    edge_copy, state_copy = copies(sems, (edge_ref, edges), (state_ref, held_ref))
    row = lax.broadcasted_iota(I32, (BORDER, PIXELS), 0)
    column = lax.broadcasted_iota(I32, (BORDER, PIXELS), 1)
    side, k, last = row // SIDE, row % SIDE, SIDE - 1
    place = jnp.where(
        side == 0,
        k,
        jnp.where(side == 1, k * SIDE + last, jnp.where(side == 2, last * SIDE + last - k, (last - k) * SIDE)),
    )
    picks = (place == column).astype(F32).astype(BF16)
    row = lax.broadcasted_iota(I32, (STRIPS, STRIPS * SIDE), 0)
    column = lax.broadcasted_iota(I32, (STRIPS, STRIPS * SIDE), 1)
    corners_ref[...] = (row * SIDE == column).astype(F32).astype(BF16)
    own, paired, near, far = neighbours(faces)
    edge_copy.wait()
    for target, start, capacity in ((paired, 0, 4), (near, 4, 2), (far, 6, 2)):
        taken = jnp.int32(0)
        for strip in range(STRIPS):
            wanted = edges[strip % 4, target * HERE + strip // 4]
            fits = jnp.logical_and(wanted >> 4 == own, taken < capacity)
            send[jnp.where(fits, start + taken, 8)] = wanted & 15
            taken = taken + fits.astype(I32)
    for slot in range(8):
        table_ref[slot] = send[slot]
    state_copy.wait()
    features = state_ref.shape[-1]
    for tile in range(HERE):
        strips = dot(picks, held_ref[tile].reshape(PIXELS, features)).astype(BF16)
        strips_ref[4 * tile : 4 * tile + 4] = strips.reshape(4, SIDE, features)
    address(strips_ref, send, near_ref, far_ref, pair_ref, corners_ref)


def side_kernel(faces, *refs):
    edge_ref, corner_ref, conv_ref, border_ref, plain_ref, tile_ref, inner_ref, ring_ref, send_ref, state_ref = refs[:10]
    table_ref, narrow1_ref, narrow2_ref, wide1_ref, wide2_ref, border_held, plain_held, tile_held, inner_held, strips_ref = refs[10:20]
    edges, cornered, conv, ring_held, sems = refs[20:]
    started = copies(
        sems,
        (edge_ref, edges),
        (corner_ref, cornered),
        (conv_ref.at[0], conv),
        (ring_ref, ring_held),
        (border_ref, border_held),
        (plain_ref, plain_held),
        (tile_ref, tile_held),
        (inner_ref, inner_held),
    )
    for weight in (narrow1_ref, narrow2_ref, wide1_ref, wide2_ref):
        weight[...] = jnp.zeros_like(weight)
    own, paired, near, far = neighbours(faces)
    from_pair, from_near, from_far = jnp.int32(0), jnp.int32(0), jnp.int32(0)
    for copy in started[:4]:
        copy.wait()
    for slot in range(8):
        table_ref[2 * STRIPS + slot] = send_ref[slot]
    for strip in range(STRIPS):
        wanted = edges[strip % 4, own * HERE + strip // 4]
        holder, place = wanted >> 4, wanted & 15
        by_pair, by_near, mine = holder == paired, holder == near, holder == own
        by_far = jnp.logical_not(mine | by_pair | by_near)
        table_ref[strip] = jnp.where(
            mine,
            place,
            jnp.where(
                by_pair,
                STRIPS + jnp.minimum(from_pair, 3),
                jnp.where(
                    by_near,
                    STRIPS + 4 + jnp.minimum(from_near, 1),
                    STRIPS + 6 + jnp.minimum(from_far, 1),
                ),
            ),
        )
        from_pair = from_pair + by_pair.astype(I32)
        from_near = from_near + by_near.astype(I32)
        from_far = from_far + by_far.astype(I32)
    for corner in range(STRIPS):
        wanted = cornered[corner % 4, own * HERE + corner // 4]
        safe = jnp.maximum(wanted, 0)
        holder, place = safe >> 4, safe & 15
        source = jnp.where(
            holder == own,
            0,
            jnp.where(
                holder == paired,
                1,
                jnp.where(holder == near, 2, jnp.where(holder == (near ^ 1), 3, jnp.where(holder == far, 4, 5))),
            ),
        )
        table_ref[STRIPS + corner] = jnp.where(wanted < 0, ZERO_ROW, source * STRIPS + place)
    for layer, (narrow, wide) in enumerate(((narrow1_ref, wide1_ref), (narrow2_ref, wide2_ref))):
        spread(conv, layer, narrow, wide)
    features = state_ref.shape[-1]
    for tile in range(HERE):
        rows = state_ref[tile, 1 : 1 + INNER].reshape(INNER * SIDE, features)
        strips_ref[4 * tile : 4 * tile + 4] = dot(ring_held[...], rows).astype(BF16).reshape(4, SIDE, features)
    for copy in started[4:]:
        copy.wait()


def spread(conv, layer, narrow, wide):
    for a in range(3):
        for b in range(3):
            tap = conv[layer, 3 * a + b]
            for level in range(2):
                lanes = 64 * level
                narrow[pl.ds(128 * (3 * a + b) + lanes, 64), pl.ds(lanes, 64)] = tap
                for parity in range(2):
                    wide[pl.ds(128 * (4 * a + b + parity) + lanes, 64), pl.ds(128 * parity + lanes, 64)] = tap


def weights_kernel(*refs):
    conv_ref, mix_in_ref, mix_out_ref, _, narrow1_ref, narrow2_ref, wide1_ref, wide2_ref, mix_in_held, mix_out_held, conv, sems = refs
    started = copies(sems, (conv_ref.at[1], conv), (mix_in_ref, mix_in_held), (mix_out_ref, mix_out_held))
    for weight in (narrow1_ref, narrow2_ref, wide1_ref, wide2_ref):
        weight[...] = jnp.zeros_like(weight)
    started[0].wait()
    for layer, (narrow, wide) in enumerate(((narrow1_ref, wide1_ref), (narrow2_ref, wide2_ref))):
        spread(conv, layer, narrow, wide)
    for copy in started[1:]:
        copy.wait()


def inner_strips(field_ref, inner_ref, strips_ref):
    features = field_ref.shape[-1]
    for pair in range(HERE // 2):
        strips = dot(inner_ref[...], field_ref[pair].reshape(2 * INNER * SIDE, features)).astype(BF16)
        strips_ref[8 * pair : 8 * pair + 8] = strips.reshape(8, SIDE, features)


def gather_rims(received, strips_ref, inner_ref, table_ref, held, corners, row, known):
    near_ref, far_ref, pair_ref, near2_ref, far2_ref = received
    features = strips_ref.shape[-1]
    for strip in range(STRIPS):
        held[strip] = strips_ref[strip]
        corners[strip : strip + 1] = strips_ref[strip, 0:1].astype(F32)
    for slot in range(4):
        held[STRIPS + slot] = pair_ref[slot]
    for slot in range(2):
        held[STRIPS + 4 + slot] = near_ref[slot]
        held[STRIPS + 6 + slot] = far_ref[slot]
    for source, ref in enumerate((pair_ref.at[4], near_ref.at[2], near2_ref.at[2], far_ref.at[2], far2_ref.at[2])):
        corners[(source + 1) * STRIPS : (source + 2) * STRIPS] = ref[...].astype(F32)
    corners[ZERO_ROW : ZERO_ROW + 8] = jnp.zeros((8, features), F32)
    row[...] = jnp.zeros_like(row)
    for tile in range(HERE):
        for side in range(4):
            strip = 4 * tile + side
            known[tile, SIDE * side : SIDE * (side + 1)] = strips_ref[strip]
            known[tile, BORDER + SIDE * side : BORDER + SIDE * (side + 1)] = inner_ref[strip]
            known[tile, 2 * BORDER + SIDE * side : 2 * BORDER + SIDE * (side + 1)] = held[table_ref[strip]]
            row[tile, side : side + 1] = corners[pl.ds(table_ref[STRIPS + strip], 1)]
        known[tile, 3 * BORDER :] = row[tile].astype(BF16)


def border_conv(received, strips_ref, inner_ref, table_ref, weight_ref, border_ref, scratch):
    held, corners, row, known, patches = scratch
    gather_rims(received, strips_ref, inner_ref, table_ref, held, corners, row, known)
    features, width = strips_ref.shape[-1], weight_ref.shape[-1]
    for tile in range(HERE):
        moved = dot(border_ref[...], known[tile]).astype(BF16)
        for tap in range(9):
            patches[tap, BORDER * tile : BORDER * (tile + 1)] = moved[BORDER * tap : BORDER * (tap + 1)]
    for group in range(features // width):
        lanes = slice(width * group, width * (group + 1))
        yield lanes, dot(jnp.concatenate([patches[tap, :, lanes] for tap in range(9)], 1), weight_ref[...])


def border_kernel(last, sends, *refs):
    strips_ref, inner_ref, *received = refs[:7]
    table_ref, weight_ref, border_ref, corners_ref = refs[7:11]
    rest = list(refs[11:])
    state_ref = rest.pop(0) if last else None
    out_ref = rest.pop(0)
    messages = [rest.pop(0) for _ in range(3 if sends else 0)]
    for lanes, total in border_conv(received, strips_ref, inner_ref, table_ref, weight_ref, border_ref, rest):
        if last:
            total = total + state_ref[:, :, lanes].reshape(total.shape).astype(F32)
        else:
            total = gelu(total)
        out_ref[:, :, lanes] = total.astype(BF16).reshape(STRIPS, SIDE, -1)
    if sends:
        address(out_ref, table_ref.at[pl.ds(2 * STRIPS, 8)], *messages, corners_ref)


def tile_conv(field_ref, strips_ref, weight_ref, tile_ref, shifted, pair):
    features = strips_ref.shape[-1]
    strips = strips_ref[8 * pair : 8 * pair + 8].reshape(2 * BORDER, features)
    for group, start in enumerate(STARTS):
        if field_ref.shape[0] == HERE:
            rows = [field_ref[2 * pair + tile, start + 1 : start + 5] for tile in range(2)]
        else:
            rows = [field_ref[pair, parity, start : start + 4] for parity in range(2)]
        known = jnp.concatenate([part.reshape(BORDER, features) for part in rows] + [strips], 0)
        moved = dot(tile_ref[group], known).astype(BF16)
        shifted[:, 4 * group : 4 * group + 4] = moved.reshape(4, 4, SIDE, features)
    for group in range(features // 128):
        lanes = slice(128 * group, 128 * (group + 1))
        windows = [shifted[c, a : a + INNER, :, lanes].reshape(INNER * SIDE, 128) for a in range(3) for c in range(4)]
        yield lanes, dot(jnp.concatenate(windows, 1), weight_ref[...])


def columns_of(total, parity):
    return total[:, 128 * parity : 128 * (parity + 1)]


def inner_kernel(field_ref, strips_ref, weight_ref, tile_ref, inner_ref, out_ref, ring_ref, *rest):
    *kept, shifted = rest
    for pair in range(HERE // 2):
        window = shifted.at[pair]
        for lanes, total in tile_conv(field_ref, strips_ref, weight_ref, tile_ref, window, pair):
            total = gelu(total).astype(BF16)
            for parity in range(2):
                out_ref[pair, parity, :, :, lanes] = columns_of(total, parity).reshape(INNER, SIDE, 128)
        for ref in kept:
            ref[pair] = window[1:3, 1 : 1 + INNER]
    inner_strips(out_ref, inner_ref, ring_ref)


def second_inner_kernel(field_ref, strips_ref, weight_ref, tile_ref, state_ref, out_ref, shifted):
    for pair in range(HERE // 2):
        for lanes, total in tile_conv(field_ref, strips_ref, weight_ref, tile_ref, shifted.at[pair], pair):
            for parity in range(2):
                before = state_ref[pair, parity, :, :, lanes].reshape(INNER * SIDE, 128)
                after = (columns_of(total, parity) + before.astype(F32)).astype(BF16)
                out_ref[pair, parity, :, :, lanes] = after.reshape(INNER, SIDE, 128)


def mixer(block, level, mix_in_ref, mix_out_ref, outs):
    levels = mix_in_ref.shape[1] // 128
    order = [level ^ back for back in range(levels)]
    first = jnp.concatenate([mix_in_ref[block, pl.ds(pl.multiple_of(128 * place, 128), 128), :] for place in order], 0)
    second = [mix_out_ref[block, :, pl.ds(pl.multiple_of(128 * place, 128), 128)] for place in order[:outs]]
    second = jnp.concatenate(second, 1) if outs > 1 else second[0]

    def mix(column):
        hidden = gelu(dot(column, first)).astype(BF16)
        return (column[:, : 128 * outs].astype(F32) + dot(hidden, second)).astype(BF16)

    return mix


def mix_strips_kernel(block, own_ref, one_ref, two_ref, three_ref, mix_in_ref, mix_out_ref, table_ref, corners_ref, strips_ref, near_ref, far_ref, pair_ref):
    mix = mixer(block, lax.axis_index("level"), mix_in_ref, mix_out_ref, 4)
    column = jnp.concatenate([ref[...].reshape(STRIPS * SIDE, 128) for ref in (own_ref, one_ref, two_ref, three_ref)], 1)
    strips_ref[...] = mix(column).reshape(STRIPS, SIDE, 512)
    address(strips_ref, table_ref.at[pl.ds(2 * STRIPS, 8)], near_ref, far_ref, pair_ref, corners_ref)


def mix_tiles_kernel(block, own_ref, one_ref, two_ref, three_ref, mix_in_ref, mix_out_ref, inner_ref, out_ref, ring_ref):
    mix = mixer(block, lax.axis_index("level"), mix_in_ref, mix_out_ref, 4)
    for pair in range(HERE // 2):
        for parity in range(2):
            parts = [ref[pair, parity].reshape(INNER * SIDE, 128) for ref in (own_ref, one_ref, two_ref, three_ref)]
            out_ref[pair, parity] = mix(jnp.concatenate(parts, 1)).reshape(INNER, SIDE, 512)
    inner_strips(out_ref, inner_ref, ring_ref)


def last_inner_kernel(block, field_ref, strips_ref, weight_ref, tile_ref, state_ref, mix_in_ref, mix_out_ref, out_ref, shifted):
    mix = mixer(block, lax.axis_index("level"), mix_in_ref, mix_out_ref, 1)
    for pair in range(HERE // 2):
        columns = [], []
        for lanes, total in tile_conv(field_ref, strips_ref, weight_ref, tile_ref, shifted.at[pair], pair):
            for parity in range(2):
                before = state_ref[pair, parity, :, :, lanes].reshape(INNER * SIDE, 128)
                columns[parity].append((columns_of(total, parity) + before.astype(F32)).astype(BF16))
        for parity in range(2):
            mixed = mix(jnp.concatenate(columns[parity], 1))
            out_ref[pair, parity] = mixed.reshape(INNER, SIDE, 128)


def last_border_kernel(block, *refs):
    strips_ref, inner_ref, *received = refs[:7]
    table_ref, weight_ref, border_ref, state_ref, mix_in_ref, mix_out_ref, tiles_ref, merge_ref, out_ref = refs[7:16]
    mix = mixer(block, lax.axis_index("level"), mix_in_ref, mix_out_ref, 1)
    columns = []
    for lanes, total in border_conv(received, strips_ref, inner_ref, table_ref, weight_ref, border_ref, refs[16:]):
        columns.append((total + state_ref[:, :, lanes].reshape(total.shape).astype(F32)).astype(BF16))
    mixed = mix(jnp.concatenate(columns, 1))
    for pair in range(HERE // 2):
        strips = mixed[2 * BORDER * pair : 2 * BORDER * (pair + 1)]
        for group, start in enumerate(STARTS):
            rows = [tiles_ref[pair, parity, start : start + 4].reshape(BORDER, 128) for parity in range(2)]
            merged = dot(merge_ref[group], jnp.concatenate(rows + [strips], 0)).astype(BF16)
            merged = merged.reshape(2, 4, SIDE, 128)
            for tile in range(2):
                out_ref[2 * pair + tile, 4 * group : 4 * group + 4] = merged[tile]


V = pl.BlockSpec(memory_space=pltpu.VMEM)
S = pl.BlockSpec(memory_space=pltpu.SMEM)
H = pl.BlockSpec(memory_space=pltpu.HBM)


def call(kernel, name, in_specs, out_specs, out_shape, scratch, args):
    return pl.pallas_call(
        kernel,
        name=name,
        in_specs=in_specs,
        out_specs=out_specs,
        out_shape=out_shape,
        scratch_shapes=scratch,
        compiler_params=pltpu.CompilerParams(vmem_limit_bytes=VMEM_LIMIT),
    )(*(pltpu.with_memory_space_constraint(arg, pltpu.HBM) if spec is H else arg for spec, arg in zip(in_specs, args)))


def arrays(*shapes):
    return [jax.ShapeDtypeStruct(shape, BF16) for shape in shapes]


def strip_shape(features):
    return STRIPS, SIDE, features


def tiles_shape(features):
    return HERE // 2, 2, INNER, SIDE, features


def message_shapes(features):
    return (3, SIDE, features), (3, SIDE, features), (5, SIDE, features)


def border_scratch(features):
    return [
        pltpu.VMEM((STRIPS + 8, SIDE, features), BF16),
        pltpu.VMEM((ZERO_ROW + 8, features), F32),
        pltpu.VMEM((HERE, SIDE, features), F32),
        pltpu.VMEM((HERE, 3 * BORDER + SIDE, features), BF16),
        pltpu.VMEM((9, STRIPS * SIDE, features), BF16),
    ]


def tile_scratch(features):
    return [pltpu.VMEM((HERE // 2, 4, SIDE, SIDE, features), BF16)]


def send(near, far, to_pair):
    faces = lax.axis_size("face")
    apart = [(i, (i + 2) % faces if i & 2 else (i - 2) % faces) for i in range(faces)]
    from_far = lax.ppermute(far, "face", apart)
    from_near = lax.ppermute(near, "face", [(i, i ^ 2) for i in range(faces)])
    return from_near, from_far, lax.ppermute(to_pair, "face", [(i, i ^ 1) for i in range(faces)])


def receive(sent, beside_near, beside_far):
    near, *beside_near = lax.optimization_barrier((sent[0], *beside_near))
    far, *beside_far = lax.optimization_barrier((sent[1], *beside_far))
    pairs = [(i, i ^ 1) for i in range(lax.axis_size("face"))]
    arrived = near, far, sent[2], lax.ppermute(near, "face", pairs), lax.ppermute(far, "face", pairs)
    return arrived, *beside_near, *beside_far


def from_level(shard, distance):
    levels = lax.axis_size("level")
    return lax.ppermute(shard, "level", [(i, i ^ distance) for i in range(levels)])


def shards(state, conv_weight, mix_in, mix_out, edge_source, corner_source):
    faces = lax.axis_size("face")
    thin = state.shape[-1]
    wide = 4 * thin
    tables = border_table(), tile_table(False), tile_table(True), paired_inner_table(), inner_table()
    border_hbm, plain_hbm, tile_hbm, inner_hbm, ring_hbm = (jnp.asarray(t) for t in tables)
    edges, cornered = edge_source.T, corner_source.T
    edge_scratch = pltpu.SMEM(edges.shape, I32)

    strips, *messages, sends, state, corners = call(
        functools.partial(first_kernel, faces), "first",
        [H, H], [V, V, V, V, S, V, V],
        arrays(strip_shape(thin), *message_shapes(thin))
        + [jax.ShapeDtypeStruct((8,), I32)]
        + arrays(state.shape, (STRIPS, STRIPS * SIDE)),
        [edge_scratch, pltpu.SMEM((16,), I32), pltpu.SemaphoreType.DMA((2,))],
        (state, edges),
    )
    sent = send(*messages)
    shape_w = (1152, 128), (1152, 128), (1536, 256), (1536, 256)
    table, narrow1, narrow2, wide1, wide2, borders, plain, tiled, inner_places, state_inner = call(
        functools.partial(side_kernel, faces), "side",
        [H] * 8 + [S, V], [S] + [V] * 9,
        [jax.ShapeDtypeStruct((2 * STRIPS + 8,), I32)]
        + arrays(*shape_w, border_hbm.shape, plain_hbm.shape, tile_hbm.shape, inner_hbm.shape, strip_shape(thin)),
        [
            edge_scratch,
            edge_scratch,
            pltpu.VMEM(conv_weight.shape[1:], BF16),
            pltpu.VMEM(ring_hbm.shape, BF16),
            pltpu.SemaphoreType.DMA((8,)),
        ],
        (edges, cornered, conv_weight, border_hbm, plain_hbm, tile_hbm, inner_hbm, ring_hbm, sends, state),
    )

    def border(last, sending, strips, inner_strips, received, weight, residual=()):
        size = strips.shape[-1]
        shapes = [strip_shape(size), *(message_shapes(size) if sending else ())]
        return call(
            functools.partial(border_kernel, last, sending), f"border_{size}_{int(last)}",
            [V] * 7 + [S] + [V] * 3 + [V] * len(residual), [V] * len(shapes),
            arrays(*shapes), border_scratch(size),
            (strips, inner_strips, *received, table, weight, borders, corners, *residual),
        )

    def interior(field, strips, weight, table, keep=False):
        size = field.shape[-1]
        shapes = [tiles_shape(size), strip_shape(size)] + ([tiles_shape(size)] if keep else [])
        return call(
            inner_kernel, f"inner_{size}",
            [V] * 5, [V] * len(shapes), arrays(*shapes), tile_scratch(size),
            (field, strips, weight, table, inner_places),
        )

    received, table = receive(sent, (), (table,))
    inner_edge, *messages = border(False, True, strips, state_inner, received, narrow1)

    sent = send(*messages)
    inner, inner_ring, before = interior(state, strips, wide1, plain, True)
    (field,) = call(
        second_inner_kernel, "inner_second", [V] * 5, [V], arrays(tiles_shape(thin)), tile_scratch(thin),
        (inner, inner_edge, wide2, tiled, before),
    )
    received, inner_ring, field = receive(sent, (inner_ring,), (field,))
    *received, field = lax.optimization_barrier((*received, field))
    one, three = from_level(field, 1), from_level(field, 3)
    (edge,) = border(True, False, inner_edge, inner_ring, received, narrow2, (strips,))

    parts = [from_level(edge, d) for d in (2, 1, 3)]
    narrow3, narrow4, wide1, wide2, mix_in, mix_out = call(
        weights_kernel, "weights", [H] * 3 + [V], [V] * 6,
        arrays(*shape_w, mix_in.shape, mix_out.shape),
        [pltpu.VMEM(conv_weight.shape[1:], BF16), pltpu.SemaphoreType.DMA((3,))],
        (conv_weight, mix_in, mix_out, edge),
    )
    *parts, mix_in, three = lax.optimization_barrier((*parts, mix_in, three))
    edge_parts = [edge, parts[1], parts[0], parts[2]]
    fields = [field, one, from_level(three, 1), three]
    strips, *messages = call(
        functools.partial(mix_strips_kernel, 0), "mix_strips",
        [V] * 6 + [S, V], [V] * 4,
        arrays(strip_shape(wide), *message_shapes(wide)), [],
        (*edge_parts, mix_in, mix_out, table, corners),
    )
    sent = send(*messages)
    field, ring1 = call(
        functools.partial(mix_tiles_kernel, 0), "mix_tiles",
        [V] * 7, [V] * 2, arrays(tiles_shape(wide), strip_shape(wide)), [],
        (*fields, mix_in, mix_out, inner_places),
    )
    received, ring1 = receive(sent, (), (ring1,))
    inner_edge, *messages = border(False, True, strips, ring1, received, narrow3)

    sent = send(*messages)
    inner, inner_ring = interior(field, strips, wide1, tiled)
    tiles = call(
        functools.partial(last_inner_kernel, 1), "last_inner",
        [V] * 7, V, arrays(tiles_shape(thin))[0], tile_scratch(wide),
        (inner, inner_edge, wide2, tiled, field, mix_in, mix_out),
    )
    received, inner_ring, tiles = receive(sent, (inner_ring,), (tiles,))
    return call(
        functools.partial(last_border_kernel, 1), "last_border",
        [V] * 7 + [S] + [V] * 7, V, arrays((HERE, SIDE, SIDE, thin))[0], border_scratch(wide),
        (inner_edge, inner_ring, *received, table, narrow4, borders, strips, mix_in, mix_out, tiles, jnp.asarray(merge_table())),
    )


def solution(mesh):
    return jax.shard_map(
        shards,
        mesh=mesh,
        in_specs=(P(("ens", "face"), None, None, "level"), P(), P(), P(), P(), P()),
        out_specs=P(("ens", "face"), None, None, "level"),
        check_vma=False,
    )
```

```python
import functools

import jax
import jax.numpy as jnp
import numpy as np
from jax import lax
from jax.experimental import pallas as pl
from jax.experimental.pallas import tpu as pltpu
from jax.sharding import PartitionSpec as P

BF16, F32, I32 = jnp.bfloat16, jnp.float32, jnp.int32
SIDE = 16
INNER = SIDE - 2
PIXELS = SIDE * SIDE
HERE = 4
STRIPS = 4 * HERE
BORDER = 4 * SIDE
ARRIVED = 16 * STRIPS
CANDIDATES = ARRIVED + (5 + 3 + 3 + 1 + 1) * SIDE
VMEM_LIMIT = 16 * 1024 * 1024


def one_hot(columns, width):
    table = np.zeros((len(columns), width), np.float32)
    for row, column in enumerate(columns):
        if column is not None:
            table[row, column] = 1.0
    return table.astype(jnp.bfloat16)


def strip_pixel(side, k, depth=0):
    last = SIDE - 1
    return ((depth, k), (k, last - depth), (last - depth, last - k), (last - k, depth))[side]


def ring(depth):
    places = {}
    for side in range(4):
        for k in range(depth, SIDE - depth):
            places.setdefault(strip_pixel(side, k, depth), SIDE * side + k)
    return places


def border_table():
    outer, inner, last = ring(0), ring(1), SIDE - 1
    corner = {(-1, -1): 0, (-1, SIDE): 1, (SIDE, SIDE): 2, (SIDE, -1): 3}
    columns = []
    for a in range(3):
        for b in range(3):
            for side in range(4):
                for k in range(SIDE):
                    i, j = strip_pixel(side, k)
                    i, j = i + a - 1, j + b - 1
                    if (i, j) in corner:
                        columns.append(3 * BORDER + corner[i, j])
                    elif i < 0:
                        columns.append(2 * BORDER + last - j)
                    elif j > last:
                        columns.append(2 * BORDER + SIDE + last - i)
                    elif i > last:
                        columns.append(2 * BORDER + 2 * SIDE + j)
                    elif j < 0:
                        columns.append(2 * BORDER + 3 * SIDE + i)
                    elif (i, j) in outer:
                        columns.append(outer[i, j])
                    else:
                        columns.append(BORDER + inner[i, j])
    return one_hot(columns, 3 * BORDER + SIDE)


STARTS = 0, 3, 7, 10


def known_rows(group, paired):
    outer, places = ring(0), {}
    for tile in range(2):
        for (i, j), place in outer.items():
            places[tile, i, j] = 2 * BORDER + BORDER * tile + place
        for row in range(4):
            for j in range(1, SIDE - 1):
                i = STARTS[group] + row + 1
                if 1 <= i < SIDE - 1:
                    apart = BORDER * (j % 2) + SIDE * row + 8 * tile + j // 2
                    places[tile, i, j] = apart if paired else BORDER * tile + SIDE * row + j
    return places


def tile_table(paired):
    groups = []
    for group in range(4):
        places, columns = known_rows(group, paired), []
        for shift in range(4):
            for i in range(4 * group, 4 * group + 4):
                for tile in range(2):
                    columns += [places.get((tile, i, 2 * n + shift - 1)) for n in range(8)]
        groups.append(one_hot(columns, 4 * BORDER))
    return np.stack(groups)


def merge_table():
    groups = []
    for group in range(4):
        places = known_rows(group, True)
        rows = range(4 * group, 4 * group + 4)
        columns = [places[tile, i, j] for tile in range(2) for i in rows for j in range(SIDE)]
        groups.append(one_hot(columns, 4 * BORDER))
    return np.stack(groups)


def inner_table():
    columns = []
    for side in range(4):
        for k in range(SIDE):
            i, j = strip_pixel(side, k, 1)
            columns.append((i - 1) * SIDE + j if 1 <= k < SIDE - 1 else None)
    return one_hot(columns, INNER * SIDE)


def paired_inner_table():
    columns = []
    for tile in range(2):
        for side in range(4):
            for k in range(SIDE):
                i, j = strip_pixel(side, k, 1)
                place = INNER * SIDE * (j % 2) + SIDE * (i - 1) + 8 * tile + j // 2
                columns.append(place if 1 <= k < SIDE - 1 else None)
    return one_hot(columns, 2 * INNER * SIDE)


def dot(a, b):
    return jnp.dot(a, b, preferred_element_type=F32)


def gelu(z):
    return z * (0.5 + 0.5 * jnp.tanh(z * (0.7978845608028654 + 0.035677408136300125 * (z * z))))


def copies(sems, *pairs):
    started = [pltpu.make_async_copy(source, target, sems.at[n]) for n, (source, target) in enumerate(pairs)]
    for copy in started:
        copy.start()
    return started


def address(strips_ref, sender_ref, near_ref, far_ref, pair_ref):
    features = strips_ref.shape[-1]
    wanted = dot(sender_ref[...], strips_ref[...].reshape(STRIPS * SIDE, features)).astype(BF16)
    wanted = wanted.reshape(11, SIDE, features)
    near_ref[...] = wanted[0:3]
    far_ref[...] = wanted[3:6]
    pair_ref[...] = wanted[6:11]


def run_of_rows(start, width):
    row = lax.broadcasted_iota(I32, (SIDE, width), 0)
    column = lax.broadcasted_iota(I32, (SIDE, width), 1)
    return (column == row + start).astype(F32).astype(BF16)


def neighbours(faces):
    own = lax.axis_index("face")
    ahead, behind = lax.rem(own + 2, faces), lax.rem(own + faces - 2, faces)
    return own, own ^ 1, own ^ 2, jnp.where(own & 2 == 0, behind, ahead)


def first_kernel(faces, state_ref, edge_ref, strips_ref, near_ref, far_ref, pair_ref, held_ref, sender_ref, edges, send, sems):
    edge_copy, state_copy = copies(sems, (edge_ref, edges), (state_ref, held_ref))
    row = lax.broadcasted_iota(I32, (BORDER, PIXELS), 0)
    column = lax.broadcasted_iota(I32, (BORDER, PIXELS), 1)
    side, k, last = row // SIDE, row % SIDE, SIDE - 1
    place = jnp.where(
        side == 0,
        k,
        jnp.where(side == 1, k * SIDE + last, jnp.where(side == 2, last * SIDE + last - k, (last - k) * SIDE)),
    )
    picks = (place == column).astype(F32).astype(BF16)
    row = lax.broadcasted_iota(I32, (STRIPS, STRIPS * SIDE), 0)
    column = lax.broadcasted_iota(I32, (STRIPS, STRIPS * SIDE), 1)
    corners = (row * SIDE == column).astype(F32).astype(BF16)
    own, paired, near, far = neighbours(faces)
    edge_copy.wait()
    for target, start, capacity in ((near, 0, 2), (far, 2, 2), (paired, 4, 4)):
        taken = jnp.int32(0)
        for strip in range(STRIPS):
            wanted = edges[strip % 4, target * HERE + strip // 4]
            fits = jnp.logical_and(wanted >> 4 == own, taken < capacity)
            send[jnp.where(fits, start + taken, 8)] = wanted & 15
            taken = taken + fits.astype(I32)
    for block in range(11):
        slot = block - block // 3 if block < 6 else block - 2
        rows = corners if block in (2, 5, 10) else run_of_rows(SIDE * send[slot], STRIPS * SIDE)
        sender_ref[SIDE * block : SIDE * (block + 1)] = rows
    state_copy.wait()
    features = state_ref.shape[-1]
    for tile in range(HERE):
        strips = dot(picks, held_ref[tile].reshape(PIXELS, features)).astype(BF16)
        strips_ref[4 * tile : 4 * tile + 4] = strips.reshape(4, SIDE, features)
    address(strips_ref, sender_ref, near_ref, far_ref, pair_ref)


def side_kernel(faces, *refs):
    edge_ref, corner_ref, conv_ref, border_ref, plain_ref, tile_ref, inner_ref, ring_ref, state_ref = refs[:9]
    gather_ref, narrow1_ref, narrow2_ref, wide1_ref, wide2_ref, border_held, plain_held, tile_held, inner_held, strips_ref = refs[9:19]
    edges, cornered, conv, ring_held, sems = refs[19:]
    started = copies(
        sems,
        (edge_ref, edges),
        (corner_ref, cornered),
        (conv_ref.at[0], conv),
        (ring_ref, ring_held),
        (border_ref, border_held),
        (plain_ref, plain_held),
        (tile_ref, tile_held),
        (inner_ref, inner_held),
    )
    for weight in (narrow1_ref, narrow2_ref, wide1_ref, wide2_ref):
        weight[...] = jnp.zeros_like(weight)
    own, paired, near, far = neighbours(faces)
    from_pair, from_near, from_far = jnp.int32(0), jnp.int32(0), jnp.int32(0)
    for copy in started[:4]:
        copy.wait()
    near_start, far_start, late_start = ARRIVED + 5 * SIDE, ARRIVED + 8 * SIDE, ARRIVED + 11 * SIDE
    row = lax.broadcasted_iota(I32, (SIDE, CANDIDATES), 0)
    column = lax.broadcasted_iota(I32, (SIDE, CANDIDATES), 1)
    for tile in range(HERE):
        corners = row < 0
        for side in range(4):
            wanted = edges[side, own * HERE + tile]
            holder, place = wanted >> 4, wanted & 15
            by_pair, by_near, mine = holder == paired, holder == near, holder == own
            by_far = jnp.logical_not(mine | by_pair | by_near)
            arrived = jnp.where(
                by_pair,
                ARRIVED + SIDE * jnp.minimum(from_pair, 3),
                jnp.where(
                    by_near,
                    near_start + SIDE * jnp.minimum(from_near, 1),
                    far_start + SIDE * jnp.minimum(from_far, 1),
                ),
            )
            start = jnp.where(mine, SIDE * place, arrived)
            gather_ref[tile, SIDE * side : SIDE * (side + 1)] = run_of_rows(start, CANDIDATES)
            from_pair = from_pair + by_pair.astype(I32)
            from_near = from_near + by_near.astype(I32)
            from_far = from_far + by_far.astype(I32)
            wanted = cornered[side, own * HERE + tile]
            safe = jnp.maximum(wanted, 0)
            holder, place = safe >> 4, safe & 15
            start = jnp.where(
                holder == paired,
                ARRIVED + 4 * SIDE,
                jnp.where(
                    holder == near,
                    near_start + 2 * SIDE,
                    jnp.where(
                        holder == far,
                        far_start + 2 * SIDE,
                        jnp.where(holder == (near ^ 1), late_start, late_start + SIDE),
                    ),
                ),
            )
            start = jnp.where(holder == own, SIDE * place, start + place)
            start = jnp.where(wanted < 0, CANDIDATES, start)
            corners = jnp.logical_or(corners, jnp.logical_and(row == side, column == start))
        gather_ref[tile, BORDER:] = corners.astype(F32).astype(BF16)
    for layer, (narrow, wide) in enumerate(((narrow1_ref, wide1_ref), (narrow2_ref, wide2_ref))):
        spread(conv, layer, narrow, wide)
    features = state_ref.shape[-1]
    for tile in range(HERE):
        rows = state_ref[tile, 1 : 1 + INNER].reshape(INNER * SIDE, features)
        strips_ref[4 * tile : 4 * tile + 4] = dot(ring_held[...], rows).astype(BF16).reshape(4, SIDE, features)
    for copy in started[4:]:
        copy.wait()


def spread(conv, layer, narrow, wide):
    for a in range(3):
        for b in range(3):
            tap = conv[layer, 3 * a + b]
            for level in range(2):
                lanes = 64 * level
                narrow[pl.ds(128 * (3 * a + b) + lanes, 64), pl.ds(lanes, 64)] = tap
                for parity in range(2):
                    wide[pl.ds(128 * (4 * a + b + parity) + lanes, 64), pl.ds(128 * parity + lanes, 64)] = tap


def weights_kernel(*refs):
    conv_ref, mix_in_ref, mix_out_ref, _, narrow1_ref, narrow2_ref, wide1_ref, wide2_ref, mix_in_held, mix_out_held, conv, sems = refs
    started = copies(sems, (conv_ref.at[1], conv), (mix_in_ref, mix_in_held), (mix_out_ref, mix_out_held))
    for weight in (narrow1_ref, narrow2_ref, wide1_ref, wide2_ref):
        weight[...] = jnp.zeros_like(weight)
    started[0].wait()
    for layer, (narrow, wide) in enumerate(((narrow1_ref, wide1_ref), (narrow2_ref, wide2_ref))):
        spread(conv, layer, narrow, wide)
    for copy in started[1:]:
        copy.wait()


def inner_strips(field_ref, inner_ref, strips_ref):
    features = field_ref.shape[-1]
    for pair in range(HERE // 2):
        strips = dot(inner_ref[...], field_ref[pair].reshape(2 * INNER * SIDE, features)).astype(BF16)
        strips_ref[8 * pair : 8 * pair + 8] = strips.reshape(8, SIDE, features)


def border_conv(received, strips_ref, inner_ref, gather_ref, weight_ref, border_ref, patches):
    near_ref, far_ref, pair_ref, near2_ref, far2_ref = received
    features = strips_ref.shape[-1]
    strips = strips_ref[...].reshape(STRIPS * SIDE, features)
    inner = inner_ref[...].reshape(STRIPS * SIDE, features)
    arrived = [ref[...].reshape(-1, features) for ref in (pair_ref, near_ref, far_ref)] + [near2_ref[2], far2_ref[2]]
    around = dot(gather_ref[...].reshape(HERE * 80, CANDIDATES), jnp.concatenate([strips] + arrived, 0)).astype(BF16)
    for tile in range(HERE):
        rows = slice(BORDER * tile, BORDER * (tile + 1))
        known = jnp.concatenate([strips[rows], inner[rows], around[80 * tile : 80 * (tile + 1)]], 0)
        moved = dot(border_ref[...], known).astype(BF16)
        for tap in range(9):
            patches[tap, rows] = moved[BORDER * tap : BORDER * (tap + 1)]
    for group in range(features // 128):
        lanes = slice(128 * group, 128 * (group + 1))
        yield lanes, dot(jnp.concatenate([patches[tap, :, lanes] for tap in range(9)], 1), weight_ref[...])


def border_kernel(last, sends, *refs):
    strips_ref, inner_ref, *received = refs[:7]
    gather_ref, weight_ref, border_ref, sender_ref = refs[7:11]
    rest = list(refs[11:])
    state_ref = rest.pop(0) if last else None
    out_ref = rest.pop(0)
    messages = [rest.pop(0) for _ in range(3 if sends else 0)]
    for lanes, total in border_conv(received, strips_ref, inner_ref, gather_ref, weight_ref, border_ref, *rest):
        if last:
            total = total + state_ref[:, :, lanes].reshape(total.shape).astype(F32)
        else:
            total = gelu(total)
        out_ref[:, :, lanes] = total.astype(BF16).reshape(STRIPS, SIDE, -1)
    if sends:
        address(out_ref, sender_ref, *messages)


def tile_conv(field_ref, strips_ref, weight_ref, tile_ref, shifted, pair):
    features = strips_ref.shape[-1]
    strips = strips_ref[8 * pair : 8 * pair + 8].reshape(2 * BORDER, features)
    for group, start in enumerate(STARTS):
        if field_ref.shape[0] == HERE:
            rows = [field_ref[2 * pair + tile, start + 1 : start + 5] for tile in range(2)]
        else:
            rows = [field_ref[pair, parity, start : start + 4] for parity in range(2)]
        known = jnp.concatenate([part.reshape(BORDER, features) for part in rows] + [strips], 0)
        moved = dot(tile_ref[group], known).astype(BF16)
        shifted[:, 4 * group : 4 * group + 4] = moved.reshape(4, 4, SIDE, features)
    for group in range(features // 128):
        lanes = slice(128 * group, 128 * (group + 1))
        windows = [shifted[c, a : a + INNER, :, lanes].reshape(INNER * SIDE, 128) for a in range(3) for c in range(4)]
        yield lanes, dot(jnp.concatenate(windows, 1), weight_ref[...])


def columns_of(total, parity):
    return total[:, 128 * parity : 128 * (parity + 1)]


def inner_kernel(field_ref, strips_ref, weight_ref, tile_ref, inner_ref, out_ref, ring_ref, *rest):
    *kept, shifted = rest
    for pair in range(HERE // 2):
        window = shifted.at[pair]
        for lanes, total in tile_conv(field_ref, strips_ref, weight_ref, tile_ref, window, pair):
            total = gelu(total).astype(BF16)
            for parity in range(2):
                out_ref[pair, parity, :, :, lanes] = columns_of(total, parity).reshape(INNER, SIDE, 128)
        for ref in kept:
            ref[pair] = window[1:3, 1 : 1 + INNER]
    inner_strips(out_ref, inner_ref, ring_ref)


def second_inner_kernel(field_ref, strips_ref, weight_ref, tile_ref, state_ref, out_ref, shifted):
    for pair in range(HERE // 2):
        for lanes, total in tile_conv(field_ref, strips_ref, weight_ref, tile_ref, shifted.at[pair], pair):
            for parity in range(2):
                before = state_ref[pair, parity, :, :, lanes].reshape(INNER * SIDE, 128)
                after = (columns_of(total, parity) + before.astype(F32)).astype(BF16)
                out_ref[pair, parity, :, :, lanes] = after.reshape(INNER, SIDE, 128)


def mixer(block, level, mix_in_ref, mix_out_ref, outs):
    levels = mix_in_ref.shape[1] // 128
    order = [level ^ back for back in range(levels)]
    first = jnp.concatenate([mix_in_ref[block, pl.ds(pl.multiple_of(128 * place, 128), 128), :] for place in order], 0)
    second = [mix_out_ref[block, :, pl.ds(pl.multiple_of(128 * place, 128), 128)] for place in order[:outs]]
    second = jnp.concatenate(second, 1) if outs > 1 else second[0]

    def mix(column):
        hidden = gelu(dot(column, first)).astype(BF16)
        return (column[:, : 128 * outs].astype(F32) + dot(hidden, second)).astype(BF16)

    return mix


def mix_strips_kernel(block, own_ref, one_ref, two_ref, three_ref, mix_in_ref, mix_out_ref, sender_ref, strips_ref, near_ref, far_ref, pair_ref):
    mix = mixer(block, lax.axis_index("level"), mix_in_ref, mix_out_ref, 4)
    column = jnp.concatenate([ref[...].reshape(STRIPS * SIDE, 128) for ref in (own_ref, one_ref, two_ref, three_ref)], 1)
    strips_ref[...] = mix(column).reshape(STRIPS, SIDE, 512)
    address(strips_ref, sender_ref, near_ref, far_ref, pair_ref)


def mix_tiles_kernel(block, own_ref, one_ref, two_ref, three_ref, mix_in_ref, mix_out_ref, inner_ref, out_ref, ring_ref):
    mix = mixer(block, lax.axis_index("level"), mix_in_ref, mix_out_ref, 4)
    for pair in range(HERE // 2):
        for parity in range(2):
            parts = [ref[pair, parity].reshape(INNER * SIDE, 128) for ref in (own_ref, one_ref, two_ref, three_ref)]
            out_ref[pair, parity] = mix(jnp.concatenate(parts, 1)).reshape(INNER, SIDE, 512)
    inner_strips(out_ref, inner_ref, ring_ref)


def last_inner_kernel(block, field_ref, strips_ref, weight_ref, tile_ref, state_ref, mix_in_ref, mix_out_ref, out_ref, shifted):
    mix = mixer(block, lax.axis_index("level"), mix_in_ref, mix_out_ref, 1)
    for pair in range(HERE // 2):
        columns = [], []
        for lanes, total in tile_conv(field_ref, strips_ref, weight_ref, tile_ref, shifted.at[pair], pair):
            for parity in range(2):
                before = state_ref[pair, parity, :, :, lanes].reshape(INNER * SIDE, 128)
                columns[parity].append((columns_of(total, parity) + before.astype(F32)).astype(BF16))
        for parity in range(2):
            mixed = mix(jnp.concatenate(columns[parity], 1))
            out_ref[pair, parity] = mixed.reshape(INNER, SIDE, 128)


def last_border_kernel(block, *refs):
    strips_ref, inner_ref, *received = refs[:7]
    gather_ref, weight_ref, border_ref, state_ref, mix_in_ref, mix_out_ref, tiles_ref, merge_ref, out_ref = refs[7:16]
    mix = mixer(block, lax.axis_index("level"), mix_in_ref, mix_out_ref, 1)
    columns = []
    for lanes, total in border_conv(received, strips_ref, inner_ref, gather_ref, weight_ref, border_ref, *refs[16:]):
        columns.append((total + state_ref[:, :, lanes].reshape(total.shape).astype(F32)).astype(BF16))
    mixed = mix(jnp.concatenate(columns, 1))
    for pair in range(HERE // 2):
        strips = mixed[2 * BORDER * pair : 2 * BORDER * (pair + 1)]
        for group, start in enumerate(STARTS):
            rows = [tiles_ref[pair, parity, start : start + 4].reshape(BORDER, 128) for parity in range(2)]
            merged = dot(merge_ref[group], jnp.concatenate(rows + [strips], 0)).astype(BF16)
            merged = merged.reshape(2, 4, SIDE, 128)
            for tile in range(2):
                out_ref[2 * pair + tile, 4 * group : 4 * group + 4] = merged[tile]


V = pl.BlockSpec(memory_space=pltpu.VMEM)
H = pl.BlockSpec(memory_space=pltpu.HBM)


def call(kernel, name, in_specs, out_specs, out_shape, scratch, args):
    return pl.pallas_call(
        kernel,
        name=name,
        in_specs=in_specs,
        out_specs=out_specs,
        out_shape=out_shape,
        scratch_shapes=scratch,
        compiler_params=pltpu.CompilerParams(vmem_limit_bytes=VMEM_LIMIT),
    )(*(pltpu.with_memory_space_constraint(arg, pltpu.HBM) if spec is H else arg for spec, arg in zip(in_specs, args)))


def arrays(*shapes):
    return [jax.ShapeDtypeStruct(shape, BF16) for shape in shapes]


def strip_shape(features):
    return STRIPS, SIDE, features


def tiles_shape(features):
    return HERE // 2, 2, INNER, SIDE, features


def message_shapes(features):
    return (3, SIDE, features), (3, SIDE, features), (5, SIDE, features)


def border_scratch(features):
    return [pltpu.VMEM((9, STRIPS * SIDE, features), BF16)]


def tile_scratch(features):
    return [pltpu.VMEM((HERE // 2, 4, SIDE, SIDE, features), BF16)]


def send(near, far, to_pair):
    faces = lax.axis_size("face")
    apart = [(i, (i + 2) % faces if i & 2 else (i - 2) % faces) for i in range(faces)]
    from_far = lax.ppermute(far, "face", apart)
    from_near = lax.ppermute(near, "face", [(i, i ^ 2) for i in range(faces)])
    return from_near, from_far, lax.ppermute(to_pair, "face", [(i, i ^ 1) for i in range(faces)])


def receive(sent, beside_near, beside_far):
    near, *beside_near = lax.optimization_barrier((sent[0], *beside_near))
    far, *beside_far = lax.optimization_barrier((sent[1], *beside_far))
    pairs = [(i, i ^ 1) for i in range(lax.axis_size("face"))]
    arrived = near, far, sent[2], lax.ppermute(near, "face", pairs), lax.ppermute(far, "face", pairs)
    return arrived, *beside_near, *beside_far


def from_level(shard, distance):
    levels = lax.axis_size("level")
    return lax.ppermute(shard, "level", [(i, i ^ distance) for i in range(levels)])


def shards(state, conv_weight, mix_in, mix_out, edge_source, corner_source):
    faces = lax.axis_size("face")
    thin = state.shape[-1]
    wide = 4 * thin
    tables = border_table(), tile_table(False), tile_table(True), paired_inner_table(), inner_table()
    border_hbm, plain_hbm, tile_hbm, inner_hbm, ring_hbm = (jnp.asarray(t) for t in tables)
    edges, cornered = edge_source.T, corner_source.T
    edge_scratch = pltpu.SMEM(edges.shape, I32)

    strips, *messages, state, sender = call(
        functools.partial(first_kernel, faces), "first",
        [H, H], [V] * 6,
        arrays(strip_shape(thin), *message_shapes(thin))
        + arrays(state.shape, (11 * SIDE, STRIPS * SIDE)),
        [edge_scratch, pltpu.SMEM((16,), I32), pltpu.SemaphoreType.DMA((2,))],
        (state, edges),
    )
    sent = send(*messages)
    shape_w = (1152, 128), (1152, 128), (1536, 256), (1536, 256)
    gatherer, narrow1, narrow2, wide1, wide2, borders, plain, tiled, inner_places, state_inner = call(
        functools.partial(side_kernel, faces), "side",
        [H] * 8 + [V], [V] * 10,
        arrays((HERE, 80, CANDIDATES), *shape_w, border_hbm.shape, plain_hbm.shape, tile_hbm.shape, inner_hbm.shape, strip_shape(thin)),
        [
            edge_scratch,
            edge_scratch,
            pltpu.VMEM(conv_weight.shape[1:], BF16),
            pltpu.VMEM(ring_hbm.shape, BF16),
            pltpu.SemaphoreType.DMA((8,)),
        ],
        (edges, cornered, conv_weight, border_hbm, plain_hbm, tile_hbm, inner_hbm, ring_hbm, state),
    )

    def border(last, sending, strips, inner_strips, received, weight, residual=()):
        size = strips.shape[-1]
        shapes = [strip_shape(size), *(message_shapes(size) if sending else ())]
        return call(
            functools.partial(border_kernel, last, sending), f"border_{size}_{int(last)}",
            [V] * (11 + len(residual)), [V] * len(shapes),
            arrays(*shapes), border_scratch(size),
            (strips, inner_strips, *received, gatherer, weight, borders, sender, *residual),
        )

    def interior(field, strips, weight, table, keep=False):
        size = field.shape[-1]
        shapes = [tiles_shape(size), strip_shape(size)] + ([tiles_shape(size)] if keep else [])
        return call(
            inner_kernel, f"inner_{size}",
            [V] * 5, [V] * len(shapes), arrays(*shapes), tile_scratch(size),
            (field, strips, weight, table, inner_places),
        )

    received, gatherer = receive(sent, (), (gatherer,))
    inner_edge, *messages = border(False, True, strips, state_inner, received, narrow1)

    sent = send(*messages)
    inner, inner_ring, before = interior(state, strips, wide1, plain, True)
    (field,) = call(
        second_inner_kernel, "inner_second", [V] * 5, [V], arrays(tiles_shape(thin)), tile_scratch(thin),
        (inner, inner_edge, wide2, tiled, before),
    )
    received, inner_ring, field = receive(sent, (inner_ring,), (field,))
    *received, field = lax.optimization_barrier((*received, field))
    one, three = from_level(field, 1), from_level(field, 3)
    (edge,) = border(True, False, inner_edge, inner_ring, received, narrow2, (strips,))

    parts = [from_level(edge, d) for d in (2, 1, 3)]
    narrow3, narrow4, wide1, wide2, mix_in, mix_out = call(
        weights_kernel, "weights", [H] * 3 + [V], [V] * 6,
        arrays(*shape_w, mix_in.shape, mix_out.shape),
        [pltpu.VMEM(conv_weight.shape[1:], BF16), pltpu.SemaphoreType.DMA((3,))],
        (conv_weight, mix_in, mix_out, edge),
    )
    *parts, mix_in, three = lax.optimization_barrier((*parts, mix_in, three))
    edge_parts = [edge, parts[1], parts[0], parts[2]]
    fields = [field, one, from_level(three, 1), three]
    strips, *messages = call(
        functools.partial(mix_strips_kernel, 0), "mix_strips",
        [V] * 7, [V] * 4,
        arrays(strip_shape(wide), *message_shapes(wide)), [],
        (*edge_parts, mix_in, mix_out, sender),
    )
    sent = send(*messages)
    field, ring1 = call(
        functools.partial(mix_tiles_kernel, 0), "mix_tiles",
        [V] * 7, [V] * 2, arrays(tiles_shape(wide), strip_shape(wide)), [],
        (*fields, mix_in, mix_out, inner_places),
    )
    received, ring1 = receive(sent, (), (ring1,))
    inner_edge, *messages = border(False, True, strips, ring1, received, narrow3)

    sent = send(*messages)
    inner, inner_ring = interior(field, strips, wide1, tiled)
    tiles = call(
        functools.partial(last_inner_kernel, 1), "last_inner",
        [V] * 7, V, arrays(tiles_shape(thin))[0], tile_scratch(wide),
        (inner, inner_edge, wide2, tiled, field, mix_in, mix_out),
    )
    received, inner_ring, tiles = receive(sent, (inner_ring,), (tiles,))
    return call(
        functools.partial(last_border_kernel, 1), "last_border",
        [V] * 15, V, arrays((HERE, SIDE, SIDE, thin))[0], border_scratch(wide),
        (inner_edge, inner_ring, *received, gatherer, narrow4, borders, strips, mix_in, mix_out, tiles, jnp.asarray(merge_table())),
    )


def solution(mesh):
    return jax.shard_map(
        shards,
        mesh=mesh,
        in_specs=(P(("ens", "face"), None, None, "level"), P(), P(), P(), P(), P()),
        out_specs=P(("ens", "face"), None, None, "level"),
        check_vma=False,
    )
```

```python
import functools

import jax
import jax.numpy as jnp
import numpy as np
from jax import lax
from jax.experimental import pallas as pl
from jax.experimental.pallas import tpu as pltpu
from jax.sharding import PartitionSpec as P

BF16, F32, I32 = jnp.bfloat16, jnp.float32, jnp.int32
SIDE = 16
INNER = SIDE - 2
PIXELS = SIDE * SIDE
HERE = 4
STRIPS = 4 * HERE
BORDER = 4 * SIDE
ARRIVED = 16 * STRIPS
CANDIDATES = ARRIVED + (5 + 3 + 3 + 1 + 1) * SIDE
VMEM_LIMIT = 16 * 1024 * 1024


def one_hot(columns, width):
    table = np.zeros((len(columns), width), np.float32)
    for row, column in enumerate(columns):
        if column is not None:
            table[row, column] = 1.0
    return table.astype(jnp.bfloat16)


def strip_pixel(side, k, depth=0):
    last = SIDE - 1
    return ((depth, k), (k, last - depth), (last - depth, last - k), (last - k, depth))[side]


def ring(depth):
    places = {}
    for side in range(4):
        for k in range(depth, SIDE - depth):
            places.setdefault(strip_pixel(side, k, depth), SIDE * side + k)
    return places


def border_table():
    outer, inner, last = ring(0), ring(1), SIDE - 1
    corner = {(-1, -1): 0, (-1, SIDE): 1, (SIDE, SIDE): 2, (SIDE, -1): 3}
    columns = []
    for a in range(3):
        for b in range(3):
            for side in range(4):
                for k in range(SIDE):
                    i, j = strip_pixel(side, k)
                    i, j = i + a - 1, j + b - 1
                    if (i, j) in corner:
                        columns.append(3 * BORDER + corner[i, j])
                    elif i < 0:
                        columns.append(2 * BORDER + last - j)
                    elif j > last:
                        columns.append(2 * BORDER + SIDE + last - i)
                    elif i > last:
                        columns.append(2 * BORDER + 2 * SIDE + j)
                    elif j < 0:
                        columns.append(2 * BORDER + 3 * SIDE + i)
                    elif (i, j) in outer:
                        columns.append(outer[i, j])
                    else:
                        columns.append(BORDER + inner[i, j])
    return one_hot(columns, 3 * BORDER + SIDE)


STARTS = 0, 3, 7, 10


def known_rows(group, paired):
    outer, places = ring(0), {}
    for tile in range(2):
        for (i, j), place in outer.items():
            places[tile, i, j] = 2 * BORDER + BORDER * tile + place
        for row in range(4):
            for j in range(1, SIDE - 1):
                i = STARTS[group] + row + 1
                if 1 <= i < SIDE - 1:
                    apart = BORDER * (j % 2) + SIDE * row + 8 * tile + j // 2
                    places[tile, i, j] = apart if paired else BORDER * tile + SIDE * row + j
    return places


def tile_table(paired):
    groups = []
    for group in range(4):
        places, columns = known_rows(group, paired), []
        for shift in range(4):
            for i in range(4 * group, 4 * group + 4):
                for tile in range(2):
                    columns += [places.get((tile, i, 2 * n + shift - 1)) for n in range(8)]
        groups.append(one_hot(columns, 4 * BORDER))
    return np.stack(groups)


def merge_table():
    groups = []
    for group in range(4):
        places = known_rows(group, True)
        rows = range(4 * group, 4 * group + 4)
        columns = [places[tile, i, j] for tile in range(2) for i in rows for j in range(SIDE)]
        groups.append(one_hot(columns, 4 * BORDER))
    return np.stack(groups)


def inner_table():
    columns = []
    for side in range(4):
        for k in range(SIDE):
            i, j = strip_pixel(side, k, 1)
            columns.append((i - 1) * SIDE + j if 1 <= k < SIDE - 1 else None)
    return one_hot(columns, INNER * SIDE)


def paired_inner_table():
    columns = []
    for tile in range(2):
        for side in range(4):
            for k in range(SIDE):
                i, j = strip_pixel(side, k, 1)
                place = INNER * SIDE * (j % 2) + SIDE * (i - 1) + 8 * tile + j // 2
                columns.append(place if 1 <= k < SIDE - 1 else None)
    return one_hot(columns, 2 * INNER * SIDE)


def dot(a, b):
    return jnp.dot(a, b, preferred_element_type=F32)


def gelu(z):
    return z * (0.5 + 0.5 * jnp.tanh(z * (0.7978845608028654 + 0.035677408136300125 * (z * z))))


def copies(sems, *pairs):
    started = [pltpu.make_async_copy(source, target, sems.at[n]) for n, (source, target) in enumerate(pairs)]
    for copy in started:
        copy.start()
    return started


def address(strips_ref, sender_ref, near_ref, far_ref, pair_ref):
    features = strips_ref.shape[-1]
    wanted = dot(sender_ref[...], strips_ref[...].reshape(STRIPS * SIDE, features)).astype(BF16)
    wanted = wanted.reshape(11, SIDE, features)
    near_ref[...] = wanted[0:3]
    far_ref[...] = wanted[3:6]
    pair_ref[...] = wanted[6:11]


def run_of_rows(start, width):
    row = lax.broadcasted_iota(I32, (SIDE, width), 0)
    column = lax.broadcasted_iota(I32, (SIDE, width), 1)
    return (column == row + start).astype(F32).astype(BF16)


def neighbours(faces):
    own = lax.axis_index("face")
    ahead, behind = lax.rem(own + 2, faces), lax.rem(own + faces - 2, faces)
    return own, own ^ 1, own ^ 2, jnp.where(own & 2 == 0, behind, ahead)


def first_kernel(faces, state_ref, edge_ref, strips_ref, near_ref, far_ref, pair_ref, held_ref, sender_ref, edges, send, sems):
    edge_copy, state_copy = copies(sems, (edge_ref, edges), (state_ref, held_ref))
    row = lax.broadcasted_iota(I32, (BORDER, PIXELS), 0)
    column = lax.broadcasted_iota(I32, (BORDER, PIXELS), 1)
    side, k, last = row // SIDE, row % SIDE, SIDE - 1
    place = jnp.where(
        side == 0,
        k,
        jnp.where(side == 1, k * SIDE + last, jnp.where(side == 2, last * SIDE + last - k, (last - k) * SIDE)),
    )
    picks = (place == column).astype(F32).astype(BF16)
    row = lax.broadcasted_iota(I32, (STRIPS, STRIPS * SIDE), 0)
    column = lax.broadcasted_iota(I32, (STRIPS, STRIPS * SIDE), 1)
    corners = (row * SIDE == column).astype(F32).astype(BF16)
    own, paired, near, far = neighbours(faces)
    edge_copy.wait()
    for target, start, capacity in ((near, 0, 2), (far, 2, 2), (paired, 4, 4)):
        taken = jnp.int32(0)
        for strip in range(STRIPS):
            wanted = edges[strip % 4, target * HERE + strip // 4]
            fits = jnp.logical_and(wanted >> 4 == own, taken < capacity)
            send[jnp.where(fits, start + taken, 8)] = wanted & 15
            taken = taken + fits.astype(I32)
    for block in range(11):
        slot = block - block // 3 if block < 6 else block - 2
        rows = corners if block in (2, 5, 10) else run_of_rows(SIDE * send[slot], STRIPS * SIDE)
        sender_ref[SIDE * block : SIDE * (block + 1)] = rows
    state_copy.wait()
    features = state_ref.shape[-1]
    for tile in range(HERE):
        strips = dot(picks, held_ref[tile].reshape(PIXELS, features)).astype(BF16)
        strips_ref[4 * tile : 4 * tile + 4] = strips.reshape(4, SIDE, features)
    address(strips_ref, sender_ref, near_ref, far_ref, pair_ref)


def side_kernel(faces, *refs):
    edge_ref, corner_ref, conv_ref, border_ref, plain_ref, tile_ref, inner_ref, ring_ref, state_ref = refs[:9]
    gather_ref, narrow1_ref, narrow2_ref, wide1_ref, wide2_ref, border_held, plain_held, tile_held, inner_held, strips_ref = refs[9:19]
    edges, cornered, conv, ring_held, sems = refs[19:]
    started = copies(
        sems,
        (edge_ref, edges),
        (corner_ref, cornered),
        (conv_ref.at[0], conv),
        (ring_ref, ring_held),
        (border_ref, border_held),
        (plain_ref, plain_held),
        (tile_ref, tile_held),
        (inner_ref, inner_held),
    )
    for weight in (narrow1_ref, narrow2_ref, wide1_ref, wide2_ref):
        weight[...] = jnp.zeros_like(weight)
    own, paired, near, far = neighbours(faces)
    from_pair, from_near, from_far = jnp.int32(0), jnp.int32(0), jnp.int32(0)
    for copy in started[:4]:
        copy.wait()
    near_start, far_start, late_start = ARRIVED + 5 * SIDE, ARRIVED + 8 * SIDE, ARRIVED + 11 * SIDE
    row = lax.broadcasted_iota(I32, (SIDE, CANDIDATES), 0)
    column = lax.broadcasted_iota(I32, (SIDE, CANDIDATES), 1)
    for tile in range(HERE):
        corners = row < 0
        for side in range(4):
            wanted = edges[side, own * HERE + tile]
            holder, place = wanted >> 4, wanted & 15
            by_pair, by_near, mine = holder == paired, holder == near, holder == own
            by_far = jnp.logical_not(mine | by_pair | by_near)
            arrived = jnp.where(
                by_pair,
                ARRIVED + SIDE * jnp.minimum(from_pair, 3),
                jnp.where(
                    by_near,
                    near_start + SIDE * jnp.minimum(from_near, 1),
                    far_start + SIDE * jnp.minimum(from_far, 1),
                ),
            )
            start = jnp.where(mine, SIDE * place, arrived)
            gather_ref[tile, SIDE * side : SIDE * (side + 1)] = run_of_rows(start, CANDIDATES)
            from_pair = from_pair + by_pair.astype(I32)
            from_near = from_near + by_near.astype(I32)
            from_far = from_far + by_far.astype(I32)
            wanted = cornered[side, own * HERE + tile]
            safe = jnp.maximum(wanted, 0)
            holder, place = safe >> 4, safe & 15
            start = jnp.where(
                holder == paired,
                ARRIVED + 4 * SIDE,
                jnp.where(
                    holder == near,
                    near_start + 2 * SIDE,
                    jnp.where(
                        holder == far,
                        far_start + 2 * SIDE,
                        jnp.where(holder == (near ^ 1), late_start, late_start + SIDE),
                    ),
                ),
            )
            start = jnp.where(holder == own, SIDE * place, start + place)
            start = jnp.where(wanted < 0, CANDIDATES, start)
            corners = jnp.logical_or(corners, jnp.logical_and(row == side, column == start))
        gather_ref[tile, BORDER:] = corners.astype(F32).astype(BF16)
    for layer, (narrow, wide) in enumerate(((narrow1_ref, wide1_ref), (narrow2_ref, wide2_ref))):
        spread(conv, layer, narrow, wide)
    features = state_ref.shape[-1]
    for tile in range(HERE):
        rows = state_ref[tile, 1 : 1 + INNER].reshape(INNER * SIDE, features)
        strips_ref[4 * tile : 4 * tile + 4] = dot(ring_held[...], rows).astype(BF16).reshape(4, SIDE, features)
    for copy in started[4:]:
        copy.wait()


def spread(conv, layer, narrow, wide):
    for a in range(3):
        for b in range(3):
            tap = conv[layer, 3 * a + b]
            for level in range(2):
                lanes = 64 * level
                narrow[pl.ds(128 * (3 * a + b) + lanes, 64), pl.ds(lanes, 64)] = tap
                for parity in range(2):
                    wide[pl.ds(128 * (4 * a + b + parity) + lanes, 64), pl.ds(128 * parity + lanes, 64)] = tap


def weights_kernel(*refs):
    conv_ref, mix_in_ref, mix_out_ref, _, narrow1_ref, narrow2_ref, wide1_ref, wide2_ref, mix_in_held, mix_out_held, conv, sems = refs
    started = copies(sems, (conv_ref.at[1], conv), (mix_in_ref, mix_in_held), (mix_out_ref, mix_out_held))
    for weight in (narrow1_ref, narrow2_ref, wide1_ref, wide2_ref):
        weight[...] = jnp.zeros_like(weight)
    started[0].wait()
    for layer, (narrow, wide) in enumerate(((narrow1_ref, wide1_ref), (narrow2_ref, wide2_ref))):
        spread(conv, layer, narrow, wide)
    for copy in started[1:]:
        copy.wait()


def inner_strips(field_ref, inner_ref, strips_ref):
    features = field_ref.shape[-1]
    for pair in range(HERE // 2):
        strips = dot(inner_ref[...], field_ref[pair].reshape(2 * INNER * SIDE, features)).astype(BF16)
        strips_ref[8 * pair : 8 * pair + 8] = strips.reshape(8, SIDE, features)


def border_conv(received, strips_ref, inner_ref, gather_ref, weight_ref, border_ref, patches):
    near_ref, far_ref, pair_ref, near2_ref, far2_ref = received
    features = strips_ref.shape[-1]
    strips = strips_ref[...].reshape(STRIPS * SIDE, features)
    inner = inner_ref[...].reshape(STRIPS * SIDE, features)
    arrived = [ref[...].reshape(-1, features) for ref in (pair_ref, near_ref, far_ref)] + [near2_ref[2], far2_ref[2]]
    around = dot(gather_ref[...].reshape(HERE * 80, CANDIDATES), jnp.concatenate([strips] + arrived, 0)).astype(BF16)
    for tile in range(HERE):
        rows = slice(BORDER * tile, BORDER * (tile + 1))
        known = jnp.concatenate([strips[rows], inner[rows], around[80 * tile : 80 * (tile + 1)]], 0)
        moved = dot(border_ref[...], known).astype(BF16)
        for tap in range(9):
            patches[tap, rows] = moved[BORDER * tap : BORDER * (tap + 1)]
    for group in range(features // 128):
        lanes = slice(128 * group, 128 * (group + 1))
        yield lanes, dot(jnp.concatenate([patches[tap, :, lanes] for tap in range(9)], 1), weight_ref[...])


def border_kernel(last, sends, *refs):
    strips_ref, inner_ref, *received = refs[:7]
    gather_ref, weight_ref, border_ref, sender_ref = refs[7:11]
    rest = list(refs[11:])
    state_ref = rest.pop(0) if last else None
    out_ref = rest.pop(0)
    messages = [rest.pop(0) for _ in range(3 if sends else 0)]
    for lanes, total in border_conv(received, strips_ref, inner_ref, gather_ref, weight_ref, border_ref, *rest):
        if last:
            total = total + state_ref[:, :, lanes].reshape(total.shape).astype(F32)
        else:
            total = gelu(total)
        out_ref[:, :, lanes] = total.astype(BF16).reshape(STRIPS, SIDE, -1)
    if sends:
        address(out_ref, sender_ref, *messages)


def tile_conv(field_ref, strips_ref, weight_ref, tile_ref, shifted, pair):
    features = strips_ref.shape[-1]
    strips = strips_ref[8 * pair : 8 * pair + 8].reshape(2 * BORDER, features)
    for group, start in enumerate(STARTS):
        if field_ref.shape[0] == HERE:
            rows = [field_ref[2 * pair + tile, start + 1 : start + 5] for tile in range(2)]
        else:
            rows = [field_ref[pair, parity, start : start + 4] for parity in range(2)]
        known = jnp.concatenate([part.reshape(BORDER, features) for part in rows] + [strips], 0)
        moved = dot(tile_ref[group], known).astype(BF16)
        shifted[:, 4 * group : 4 * group + 4] = moved.reshape(4, 4, SIDE, features)
    for group in range(features // 128):
        lanes = slice(128 * group, 128 * (group + 1))
        windows = [shifted[c, a : a + INNER, :, lanes].reshape(INNER * SIDE, 128) for a in range(3) for c in range(4)]
        yield lanes, dot(jnp.concatenate(windows, 1), weight_ref[...])


def columns_of(total, parity):
    return total[:, 128 * parity : 128 * (parity + 1)]


def inner_kernel(field_ref, strips_ref, weight_ref, tile_ref, inner_ref, out_ref, ring_ref, *rest):
    *kept, shifted = rest
    for pair in range(HERE // 2):
        window = shifted.at[pair]
        for lanes, total in tile_conv(field_ref, strips_ref, weight_ref, tile_ref, window, pair):
            total = gelu(total).astype(BF16)
            for parity in range(2):
                out_ref[pair, parity, :, :, lanes] = columns_of(total, parity).reshape(INNER, SIDE, 128)
        for ref in kept:
            ref[pair] = window[1:3, 1 : 1 + INNER]
    inner_strips(out_ref, inner_ref, ring_ref)


def second_inner_kernel(field_ref, strips_ref, weight_ref, tile_ref, state_ref, out_ref, shifted):
    for pair in range(HERE // 2):
        for lanes, total in tile_conv(field_ref, strips_ref, weight_ref, tile_ref, shifted.at[pair], pair):
            for parity in range(2):
                before = state_ref[pair, parity, :, :, lanes].reshape(INNER * SIDE, 128)
                after = (columns_of(total, parity) + before.astype(F32)).astype(BF16)
                out_ref[pair, parity, :, :, lanes] = after.reshape(INNER, SIDE, 128)


def mixer(block, level, mix_in_ref, mix_out_ref, outs):
    levels = mix_in_ref.shape[1] // 128
    order = [level ^ back for back in range(levels)]
    first = jnp.concatenate([mix_in_ref[block, pl.ds(pl.multiple_of(128 * place, 128), 128), :] for place in order], 0)
    second = [mix_out_ref[block, :, pl.ds(pl.multiple_of(128 * place, 128), 128)] for place in order[:outs]]
    second = jnp.concatenate(second, 1) if outs > 1 else second[0]

    def mix(column):
        hidden = gelu(dot(column, first)).astype(BF16)
        return (column[:, : 128 * outs].astype(F32) + dot(hidden, second)).astype(BF16)

    return mix


def mix_strips_kernel(block, own_ref, one_ref, two_ref, three_ref, mix_in_ref, mix_out_ref, sender_ref, strips_ref, near_ref, far_ref, pair_ref):
    mix = mixer(block, lax.axis_index("level"), mix_in_ref, mix_out_ref, 4)
    column = jnp.concatenate([ref[...].reshape(STRIPS * SIDE, 128) for ref in (own_ref, one_ref, two_ref, three_ref)], 1)
    strips_ref[...] = mix(column).reshape(STRIPS, SIDE, 512)
    address(strips_ref, sender_ref, near_ref, far_ref, pair_ref)


def mix_tiles_kernel(block, own_ref, one_ref, two_ref, three_ref, mix_in_ref, mix_out_ref, inner_ref, out_ref, ring_ref):
    mix = mixer(block, lax.axis_index("level"), mix_in_ref, mix_out_ref, 4)
    for pair in range(HERE // 2):
        for parity in range(2):
            parts = [ref[pair, parity].reshape(INNER * SIDE, 128) for ref in (own_ref, one_ref, two_ref, three_ref)]
            out_ref[pair, parity] = mix(jnp.concatenate(parts, 1)).reshape(INNER, SIDE, 512)
    inner_strips(out_ref, inner_ref, ring_ref)


def last_inner_kernel(block, field_ref, strips_ref, weight_ref, tile_ref, state_ref, mix_in_ref, mix_out_ref, out_ref, shifted):
    mix = mixer(block, lax.axis_index("level"), mix_in_ref, mix_out_ref, 1)
    for pair in range(HERE // 2):
        columns = [], []
        for lanes, total in tile_conv(field_ref, strips_ref, weight_ref, tile_ref, shifted.at[pair], pair):
            for parity in range(2):
                before = state_ref[pair, parity, :, :, lanes].reshape(INNER * SIDE, 128)
                columns[parity].append((columns_of(total, parity) + before.astype(F32)).astype(BF16))
        for parity in range(2):
            mixed = mix(jnp.concatenate(columns[parity], 1))
            out_ref[pair, parity] = mixed.reshape(INNER, SIDE, 128)


def last_border_kernel(block, *refs):
    strips_ref, inner_ref, *received = refs[:7]
    gather_ref, weight_ref, border_ref, state_ref, mix_in_ref, mix_out_ref, tiles_ref, merge_ref, out_ref = refs[7:16]
    mix = mixer(block, lax.axis_index("level"), mix_in_ref, mix_out_ref, 1)
    columns = []
    for lanes, total in border_conv(received, strips_ref, inner_ref, gather_ref, weight_ref, border_ref, refs[16]):
        columns.append((total + state_ref[:, :, lanes].reshape(total.shape).astype(F32)).astype(BF16))
    held, sems = refs[17:]
    leaving = []
    mixed = mix(jnp.concatenate(columns, 1))
    for pair in range(HERE // 2):
        strips = mixed[2 * BORDER * pair : 2 * BORDER * (pair + 1)]
        for group, start in enumerate(STARTS):
            rows = [tiles_ref[pair, parity, start : start + 4].reshape(BORDER, 128) for parity in range(2)]
            merged = dot(merge_ref[group], jnp.concatenate(rows + [strips], 0)).astype(BF16)
            merged = merged.reshape(2, 4, SIDE, 128)
            for tile in range(2):
                held[2 * pair + tile, 4 * group : 4 * group + 4] = merged[tile]
        done = held.at[pl.ds(2 * pair, 2)], out_ref.at[pl.ds(2 * pair, 2)]
        leaving += copies(sems.at[pl.ds(pair, 1)], done)
    for copy in leaving:
        copy.wait()


V = pl.BlockSpec(memory_space=pltpu.VMEM)
H = pl.BlockSpec(memory_space=pltpu.HBM)


def call(kernel, name, in_specs, out_specs, out_shape, scratch, args):
    return pl.pallas_call(
        kernel,
        name=name,
        in_specs=in_specs,
        out_specs=out_specs,
        out_shape=out_shape,
        scratch_shapes=scratch,
        compiler_params=pltpu.CompilerParams(vmem_limit_bytes=VMEM_LIMIT),
    )(*(pltpu.with_memory_space_constraint(arg, pltpu.HBM) if spec is H else arg for spec, arg in zip(in_specs, args)))


def arrays(*shapes):
    return [jax.ShapeDtypeStruct(shape, BF16) for shape in shapes]


def strip_shape(features):
    return STRIPS, SIDE, features


def tiles_shape(features):
    return HERE // 2, 2, INNER, SIDE, features


def message_shapes(features):
    return (3, SIDE, features), (3, SIDE, features), (5, SIDE, features)


def border_scratch(features):
    return [pltpu.VMEM((9, STRIPS * SIDE, features), BF16)]


def tile_scratch(features):
    return [pltpu.VMEM((HERE // 2, 4, SIDE, SIDE, features), BF16)]


def send(near, far, to_pair):
    faces = lax.axis_size("face")
    apart = [(i, (i + 2) % faces if i & 2 else (i - 2) % faces) for i in range(faces)]
    from_far = lax.ppermute(far, "face", apart)
    from_near = lax.ppermute(near, "face", [(i, i ^ 2) for i in range(faces)])
    return from_near, from_far, lax.ppermute(to_pair, "face", [(i, i ^ 1) for i in range(faces)])


def receive(sent, beside_near, beside_far):
    near, *beside_near = lax.optimization_barrier((sent[0], *beside_near))
    far, *beside_far = lax.optimization_barrier((sent[1], *beside_far))
    pairs = [(i, i ^ 1) for i in range(lax.axis_size("face"))]
    arrived = near, far, sent[2], lax.ppermute(near, "face", pairs), lax.ppermute(far, "face", pairs)
    return arrived, *beside_near, *beside_far


def from_level(shard, distance):
    levels = lax.axis_size("level")
    return lax.ppermute(shard, "level", [(i, i ^ distance) for i in range(levels)])


def shards(state, conv_weight, mix_in, mix_out, edge_source, corner_source):
    faces = lax.axis_size("face")
    thin = state.shape[-1]
    wide = 4 * thin
    tables = border_table(), tile_table(False), tile_table(True), paired_inner_table(), inner_table()
    border_hbm, plain_hbm, tile_hbm, inner_hbm, ring_hbm = (jnp.asarray(t) for t in tables)
    edges, cornered = edge_source.T, corner_source.T
    edge_scratch = pltpu.SMEM(edges.shape, I32)

    strips, *messages, state, sender = call(
        functools.partial(first_kernel, faces), "first",
        [H, H], [V] * 6,
        arrays(strip_shape(thin), *message_shapes(thin))
        + arrays(state.shape, (11 * SIDE, STRIPS * SIDE)),
        [edge_scratch, pltpu.SMEM((16,), I32), pltpu.SemaphoreType.DMA((2,))],
        (state, edges),
    )
    sent = send(*messages)
    shape_w = (1152, 128), (1152, 128), (1536, 256), (1536, 256)
    gatherer, narrow1, narrow2, wide1, wide2, borders, plain, tiled, inner_places, state_inner = call(
        functools.partial(side_kernel, faces), "side",
        [H] * 8 + [V], [V] * 10,
        arrays((HERE, 80, CANDIDATES), *shape_w, border_hbm.shape, plain_hbm.shape, tile_hbm.shape, inner_hbm.shape, strip_shape(thin)),
        [
            edge_scratch,
            edge_scratch,
            pltpu.VMEM(conv_weight.shape[1:], BF16),
            pltpu.VMEM(ring_hbm.shape, BF16),
            pltpu.SemaphoreType.DMA((8,)),
        ],
        (edges, cornered, conv_weight, border_hbm, plain_hbm, tile_hbm, inner_hbm, ring_hbm, state),
    )

    def border(last, sending, strips, inner_strips, received, weight, residual=()):
        size = strips.shape[-1]
        shapes = [strip_shape(size), *(message_shapes(size) if sending else ())]
        return call(
            functools.partial(border_kernel, last, sending), f"border_{size}_{int(last)}",
            [V] * (11 + len(residual)), [V] * len(shapes),
            arrays(*shapes), border_scratch(size),
            (strips, inner_strips, *received, gatherer, weight, borders, sender, *residual),
        )

    def interior(field, strips, weight, table, keep=False):
        size = field.shape[-1]
        shapes = [tiles_shape(size), strip_shape(size)] + ([tiles_shape(size)] if keep else [])
        return call(
            inner_kernel, f"inner_{size}",
            [V] * 5, [V] * len(shapes), arrays(*shapes), tile_scratch(size),
            (field, strips, weight, table, inner_places),
        )

    received, gatherer = receive(sent, (), (gatherer,))
    inner_edge, *messages = border(False, True, strips, state_inner, received, narrow1)

    sent = send(*messages)
    inner, inner_ring, before = interior(state, strips, wide1, plain, True)
    (field,) = call(
        second_inner_kernel, "inner_second", [V] * 5, [V], arrays(tiles_shape(thin)), tile_scratch(thin),
        (inner, inner_edge, wide2, tiled, before),
    )
    received, inner_ring, field = receive(sent, (inner_ring,), (field,))
    *received, field = lax.optimization_barrier((*received, field))
    one, three = from_level(field, 1), from_level(field, 3)
    (edge,) = border(True, False, inner_edge, inner_ring, received, narrow2, (strips,))

    parts = [from_level(edge, d) for d in (2, 1, 3)]
    narrow3, narrow4, wide1, wide2, mix_in, mix_out = call(
        weights_kernel, "weights", [H] * 3 + [V], [V] * 6,
        arrays(*shape_w, mix_in.shape, mix_out.shape),
        [pltpu.VMEM(conv_weight.shape[1:], BF16), pltpu.SemaphoreType.DMA((3,))],
        (conv_weight, mix_in, mix_out, edge),
    )
    *parts, mix_in, three = lax.optimization_barrier((*parts, mix_in, three))
    edge_parts = [edge, parts[1], parts[0], parts[2]]
    fields = [field, one, from_level(three, 1), three]
    strips, *messages = call(
        functools.partial(mix_strips_kernel, 0), "mix_strips",
        [V] * 7, [V] * 4,
        arrays(strip_shape(wide), *message_shapes(wide)), [],
        (*edge_parts, mix_in, mix_out, sender),
    )
    sent = send(*messages)
    field, ring1 = call(
        functools.partial(mix_tiles_kernel, 0), "mix_tiles",
        [V] * 7, [V] * 2, arrays(tiles_shape(wide), strip_shape(wide)), [],
        (*fields, mix_in, mix_out, inner_places),
    )
    received, ring1 = receive(sent, (), (ring1,))
    inner_edge, *messages = border(False, True, strips, ring1, received, narrow3)

    sent = send(*messages)
    inner, inner_ring = interior(field, strips, wide1, tiled)
    tiles = call(
        functools.partial(last_inner_kernel, 1), "last_inner",
        [V] * 7, V, arrays(tiles_shape(thin))[0], tile_scratch(wide),
        (inner, inner_edge, wide2, tiled, field, mix_in, mix_out),
    )
    received, inner_ring, tiles = receive(sent, (inner_ring,), (tiles,))
    return call(
        functools.partial(last_border_kernel, 1), "last_border",
        [V] * 15, H, arrays((HERE, SIDE, SIDE, thin))[0],
        border_scratch(wide) + [pltpu.VMEM((HERE, SIDE, SIDE, thin), BF16), pltpu.SemaphoreType.DMA((2,))],
        (inner_edge, inner_ring, *received, gatherer, narrow4, borders, strips, mix_in, mix_out, tiles, jnp.asarray(merge_table())),
    )


def solution(mesh):
    return jax.shard_map(
        shards,
        mesh=mesh,
        in_specs=(P(("ens", "face"), None, None, "level"), P(), P(), P(), P(), P()),
        out_specs=P(("ens", "face"), None, None, "level"),
        check_vma=False,
    )
```

```python
import functools

import jax
import jax.numpy as jnp
import numpy as np
from jax import lax
from jax.experimental import pallas as pl
from jax.experimental.pallas import tpu as pltpu
from jax.sharding import PartitionSpec as P

BF16, F32, I32 = jnp.bfloat16, jnp.float32, jnp.int32
SIDE = 16
INNER = SIDE - 2
PIXELS = SIDE * SIDE
HERE = 4
STRIPS = 4 * HERE
BORDER = 4 * SIDE
ARRIVED = 16 * STRIPS
CANDIDATES = ARRIVED + (5 + 3 + 3 + 1 + 1) * SIDE
VMEM_LIMIT = 16 * 1024 * 1024


def one_hot(columns, width):
    table = np.zeros((len(columns), width), np.float32)
    for row, column in enumerate(columns):
        if column is not None:
            table[row, column] = 1.0
    return table.astype(jnp.bfloat16)


def strip_pixel(side, k, depth=0):
    last = SIDE - 1
    return ((depth, k), (k, last - depth), (last - depth, last - k), (last - k, depth))[side]


def ring(depth):
    places = {}
    for side in range(4):
        for k in range(depth, SIDE - depth):
            places.setdefault(strip_pixel(side, k, depth), SIDE * side + k)
    return places


def border_table():
    outer, inner, last = ring(0), ring(1), SIDE - 1
    corner = {(-1, -1): 0, (-1, SIDE): 1, (SIDE, SIDE): 2, (SIDE, -1): 3}
    columns = []
    for a in range(3):
        for b in range(3):
            for side in range(4):
                for k in range(SIDE):
                    i, j = strip_pixel(side, k)
                    i, j = i + a - 1, j + b - 1
                    if (i, j) in corner:
                        columns.append(3 * BORDER + corner[i, j])
                    elif i < 0:
                        columns.append(2 * BORDER + last - j)
                    elif j > last:
                        columns.append(2 * BORDER + SIDE + last - i)
                    elif i > last:
                        columns.append(2 * BORDER + 2 * SIDE + j)
                    elif j < 0:
                        columns.append(2 * BORDER + 3 * SIDE + i)
                    elif (i, j) in outer:
                        columns.append(outer[i, j])
                    else:
                        columns.append(BORDER + inner[i, j])
    return one_hot(columns, 3 * BORDER + SIDE)


STARTS = 0, 3, 7, 10


def known_rows(group, paired):
    outer, places = ring(0), {}
    for tile in range(2):
        for (i, j), place in outer.items():
            places[tile, i, j] = 2 * BORDER + BORDER * tile + place
        for row in range(4):
            for j in range(1, SIDE - 1):
                i = STARTS[group] + row + 1
                if 1 <= i < SIDE - 1:
                    apart = BORDER * (j % 2) + SIDE * row + 8 * tile + j // 2
                    places[tile, i, j] = apart if paired else BORDER * tile + SIDE * row + j
    return places


def tile_table(paired):
    groups = []
    for group in range(4):
        places, columns = known_rows(group, paired), []
        for shift in range(4):
            for i in range(4 * group, 4 * group + 4):
                for tile in range(2):
                    columns += [places.get((tile, i, 2 * n + shift - 1)) for n in range(8)]
        groups.append(one_hot(columns, 4 * BORDER))
    return np.stack(groups)


def merge_table():
    groups = []
    for group in range(4):
        places = known_rows(group, True)
        rows = range(4 * group, 4 * group + 4)
        columns = [places[tile, i, j] for tile in range(2) for i in rows for j in range(SIDE)]
        groups.append(one_hot(columns, 4 * BORDER))
    return np.stack(groups)


def inner_table():
    columns = []
    for side in range(4):
        for k in range(SIDE):
            i, j = strip_pixel(side, k, 1)
            columns.append((i - 1) * SIDE + j if 1 <= k < SIDE - 1 else None)
    return one_hot(columns, INNER * SIDE)


def paired_inner_table():
    columns = []
    for tile in range(2):
        for side in range(4):
            for k in range(SIDE):
                i, j = strip_pixel(side, k, 1)
                place = INNER * SIDE * (j % 2) + SIDE * (i - 1) + 8 * tile + j // 2
                columns.append(place if 1 <= k < SIDE - 1 else None)
    return one_hot(columns, 2 * INNER * SIDE)


def dot(a, b):
    return jnp.dot(a, b, preferred_element_type=F32)


def gelu(z):
    return z * (0.5 + 0.5 * jnp.tanh(z * (0.7978845608028654 + 0.035677408136300125 * (z * z))))


def copies(sems, *pairs):
    started = [pltpu.make_async_copy(source, target, sems.at[n]) for n, (source, target) in enumerate(pairs)]
    for copy in started:
        copy.start()
    return started


def address(strips_ref, sender_ref, near_ref, far_ref, pair_ref):
    features = strips_ref.shape[-1]
    wanted = dot(sender_ref[...], strips_ref[...].reshape(STRIPS * SIDE, features)).astype(BF16)
    wanted = wanted.reshape(11, SIDE, features)
    near_ref[...] = wanted[0:3]
    far_ref[...] = wanted[3:6]
    pair_ref[...] = wanted[6:11]


def run_of_rows(start, width):
    row = lax.broadcasted_iota(I32, (SIDE, width), 0)
    column = lax.broadcasted_iota(I32, (SIDE, width), 1)
    return (column == row + start).astype(F32).astype(BF16)


def neighbours(faces):
    own = lax.axis_index("face")
    ahead, behind = lax.rem(own + 2, faces), lax.rem(own + faces - 2, faces)
    return own, own ^ 1, own ^ 2, jnp.where(own & 2 == 0, behind, ahead)


def first_kernel(faces, state_ref, edge_ref, strips_ref, near_ref, far_ref, pair_ref, held_ref, sender_ref, edges, send, sems):
    edge_copy, state_copy = copies(sems, (edge_ref, edges), (state_ref, held_ref))
    row = lax.broadcasted_iota(I32, (BORDER, PIXELS), 0)
    column = lax.broadcasted_iota(I32, (BORDER, PIXELS), 1)
    side, k, last = row // SIDE, row % SIDE, SIDE - 1
    place = jnp.where(
        side == 0,
        k,
        jnp.where(side == 1, k * SIDE + last, jnp.where(side == 2, last * SIDE + last - k, (last - k) * SIDE)),
    )
    picks = (place == column).astype(F32).astype(BF16)
    row = lax.broadcasted_iota(I32, (STRIPS, STRIPS * SIDE), 0)
    column = lax.broadcasted_iota(I32, (STRIPS, STRIPS * SIDE), 1)
    corners = (row * SIDE == column).astype(F32).astype(BF16)
    own, paired, near, far = neighbours(faces)
    edge_copy.wait()
    for target, start, capacity in ((near, 0, 2), (far, 2, 2), (paired, 4, 4)):
        taken = jnp.int32(0)
        for strip in range(STRIPS):
            wanted = edges[strip % 4, target * HERE + strip // 4]
            fits = jnp.logical_and(wanted >> 4 == own, taken < capacity)
            send[jnp.where(fits, start + taken, 8)] = wanted & 15
            taken = taken + fits.astype(I32)
    for block in range(11):
        slot = block - block // 3 if block < 6 else block - 2
        rows = corners if block in (2, 5, 10) else run_of_rows(SIDE * send[slot], STRIPS * SIDE)
        sender_ref[SIDE * block : SIDE * (block + 1)] = rows
    state_copy.wait()
    features = state_ref.shape[-1]
    for tile in range(HERE):
        strips = dot(picks, held_ref[tile].reshape(PIXELS, features)).astype(BF16)
        strips_ref[4 * tile : 4 * tile + 4] = strips.reshape(4, SIDE, features)
    address(strips_ref, sender_ref, near_ref, far_ref, pair_ref)


def side_kernel(faces, *refs):
    edge_ref, corner_ref, conv_ref, border_ref, plain_ref, tile_ref, inner_ref, ring_ref, state_ref = refs[:9]
    gather_ref, narrow1_ref, narrow2_ref, wide1_ref, wide2_ref, border_held, plain_held, tile_held, inner_held, strips_ref = refs[9:19]
    edges, cornered, conv, ring_held, sems = refs[19:]
    started = copies(
        sems,
        (edge_ref, edges),
        (corner_ref, cornered),
        (conv_ref.at[0], conv),
        (ring_ref, ring_held),
        (border_ref, border_held),
        (plain_ref, plain_held),
        (tile_ref, tile_held),
        (inner_ref, inner_held),
    )
    for weight in (narrow1_ref, narrow2_ref, wide1_ref, wide2_ref):
        weight[...] = jnp.zeros_like(weight)
    own, paired, near, far = neighbours(faces)
    from_pair, from_near, from_far = jnp.int32(0), jnp.int32(0), jnp.int32(0)
    for copy in started[:4]:
        copy.wait()
    near_start, far_start, late_start = ARRIVED + 5 * SIDE, ARRIVED + 8 * SIDE, ARRIVED + 11 * SIDE
    row = lax.broadcasted_iota(I32, (SIDE, CANDIDATES), 0)
    column = lax.broadcasted_iota(I32, (SIDE, CANDIDATES), 1)
    for tile in range(HERE):
        corners = row < 0
        for side in range(4):
            wanted = edges[side, own * HERE + tile]
            holder, place = wanted >> 4, wanted & 15
            by_pair, by_near, mine = holder == paired, holder == near, holder == own
            by_far = jnp.logical_not(mine | by_pair | by_near)
            arrived = jnp.where(
                by_pair,
                ARRIVED + SIDE * jnp.minimum(from_pair, 3),
                jnp.where(
                    by_near,
                    near_start + SIDE * jnp.minimum(from_near, 1),
                    far_start + SIDE * jnp.minimum(from_far, 1),
                ),
            )
            start = jnp.where(mine, SIDE * place, arrived)
            gather_ref[tile, SIDE * side : SIDE * (side + 1)] = run_of_rows(start, CANDIDATES)
            from_pair = from_pair + by_pair.astype(I32)
            from_near = from_near + by_near.astype(I32)
            from_far = from_far + by_far.astype(I32)
            wanted = cornered[side, own * HERE + tile]
            safe = jnp.maximum(wanted, 0)
            holder, place = safe >> 4, safe & 15
            start = jnp.where(
                holder == paired,
                ARRIVED + 4 * SIDE,
                jnp.where(
                    holder == near,
                    near_start + 2 * SIDE,
                    jnp.where(
                        holder == far,
                        far_start + 2 * SIDE,
                        jnp.where(holder == (near ^ 1), late_start, late_start + SIDE),
                    ),
                ),
            )
            start = jnp.where(holder == own, SIDE * place, start + place)
            start = jnp.where(wanted < 0, CANDIDATES, start)
            corners = jnp.logical_or(corners, jnp.logical_and(row == side, column == start))
        gather_ref[tile, BORDER:] = corners.astype(F32).astype(BF16)
    for layer, (narrow, wide) in enumerate(((narrow1_ref, wide1_ref), (narrow2_ref, wide2_ref))):
        spread(conv, layer, narrow, wide)
    features = state_ref.shape[-1]
    for tile in range(HERE):
        rows = state_ref[tile, 1 : 1 + INNER].reshape(INNER * SIDE, features)
        strips_ref[4 * tile : 4 * tile + 4] = dot(ring_held[...], rows).astype(BF16).reshape(4, SIDE, features)
    for copy in started[4:]:
        copy.wait()


def spread(conv, layer, narrow, wide):
    for a in range(3):
        for b in range(3):
            tap = conv[layer, 3 * a + b]
            for level in range(2):
                lanes = 64 * level
                narrow[pl.ds(128 * (3 * a + b) + lanes, 64), pl.ds(lanes, 64)] = tap
                for parity in range(2):
                    wide[pl.ds(128 * (4 * a + b + parity) + lanes, 64), pl.ds(128 * parity + lanes, 64)] = tap


def weights_kernel(*refs):
    conv_ref, mix_in_ref, mix_out_ref, _, narrow1_ref, narrow2_ref, wide1_ref, wide2_ref, mix_in_held, mix_out_held, conv, sems = refs
    started = copies(sems, (conv_ref.at[1], conv), (mix_in_ref, mix_in_held), (mix_out_ref, mix_out_held))
    for weight in (narrow1_ref, narrow2_ref, wide1_ref, wide2_ref):
        weight[...] = jnp.zeros_like(weight)
    started[0].wait()
    for layer, (narrow, wide) in enumerate(((narrow1_ref, wide1_ref), (narrow2_ref, wide2_ref))):
        spread(conv, layer, narrow, wide)
    for copy in started[1:]:
        copy.wait()


def inner_strips(field_ref, inner_ref, strips_ref):
    features = field_ref.shape[-1]
    for pair in range(HERE // 2):
        strips = dot(inner_ref[...], field_ref[pair].reshape(2 * INNER * SIDE, features)).astype(BF16)
        strips_ref[8 * pair : 8 * pair + 8] = strips.reshape(8, SIDE, features)


def border_conv(received, strips_ref, inner_ref, gather_ref, weight_ref, border_ref, patches):
    near_ref, far_ref, pair_ref, near2_ref, far2_ref = received
    features = strips_ref.shape[-1]
    strips = strips_ref[...].reshape(STRIPS * SIDE, features)
    inner = inner_ref[...].reshape(STRIPS * SIDE, features)
    arrived = [ref[...].reshape(-1, features) for ref in (pair_ref, near_ref, far_ref)] + [near2_ref[2], far2_ref[2]]
    around = dot(gather_ref[...].reshape(HERE * 80, CANDIDATES), jnp.concatenate([strips] + arrived, 0)).astype(BF16)
    for tile in range(HERE):
        rows = slice(BORDER * tile, BORDER * (tile + 1))
        known = jnp.concatenate([strips[rows], inner[rows], around[80 * tile : 80 * (tile + 1)]], 0)
        moved = dot(border_ref[...], known).astype(BF16)
        for tap in range(9):
            patches[tap, rows] = moved[BORDER * tap : BORDER * (tap + 1)]
    for group in range(features // 128):
        lanes = slice(128 * group, 128 * (group + 1))
        yield lanes, dot(jnp.concatenate([patches[tap, :, lanes] for tap in range(9)], 1), weight_ref[...])


def border_kernel(last, sends, *refs):
    strips_ref, inner_ref, *received = refs[:7]
    gather_ref, weight_ref, border_ref, sender_ref = refs[7:11]
    rest = list(refs[11:])
    state_ref = rest.pop(0) if last else None
    out_ref = rest.pop(0)
    messages = [rest.pop(0) for _ in range(3 if sends else 0)]
    for lanes, total in border_conv(received, strips_ref, inner_ref, gather_ref, weight_ref, border_ref, *rest):
        if last:
            total = total + state_ref[:, :, lanes].reshape(total.shape).astype(F32)
        else:
            total = gelu(total)
        out_ref[:, :, lanes] = total.astype(BF16).reshape(STRIPS, SIDE, -1)
    if sends:
        address(out_ref, sender_ref, *messages)


def tile_conv(field_ref, strips_ref, weight_ref, tile_ref, shifted, pair):
    features = strips_ref.shape[-1]
    strips = strips_ref[8 * pair : 8 * pair + 8].reshape(2 * BORDER, features)
    for group, start in enumerate(STARTS):
        if field_ref.shape[0] == HERE:
            rows = [field_ref[2 * pair + tile, start + 1 : start + 5] for tile in range(2)]
        else:
            rows = [field_ref[pair, parity, start : start + 4] for parity in range(2)]
        known = jnp.concatenate([part.reshape(BORDER, features) for part in rows] + [strips], 0)
        moved = dot(tile_ref[group], known).astype(BF16)
        shifted[:, 4 * group : 4 * group + 4] = moved.reshape(4, 4, SIDE, features)
    for group in range(features // 128):
        lanes = slice(128 * group, 128 * (group + 1))
        windows = [shifted[c, a : a + INNER, :, lanes].reshape(INNER * SIDE, 128) for a in range(3) for c in range(4)]
        yield lanes, dot(jnp.concatenate(windows, 1), weight_ref[...])


def columns_of(total, parity):
    return total[:, 128 * parity : 128 * (parity + 1)]


def inner_kernel(field_ref, strips_ref, weight_ref, tile_ref, inner_ref, out_ref, ring_ref, *rest):
    *kept, shifted = rest
    for pair in range(HERE // 2):
        window = shifted.at[pair]
        for lanes, total in tile_conv(field_ref, strips_ref, weight_ref, tile_ref, window, pair):
            total = gelu(total).astype(BF16)
            for parity in range(2):
                out_ref[pair, parity, :, :, lanes] = columns_of(total, parity).reshape(INNER, SIDE, 128)
        for ref in kept:
            ref[pair] = window[1:3, 1 : 1 + INNER]
    inner_strips(out_ref, inner_ref, ring_ref)


def second_inner_kernel(field_ref, strips_ref, weight_ref, tile_ref, state_ref, out_ref, shifted):
    for pair in range(HERE // 2):
        for lanes, total in tile_conv(field_ref, strips_ref, weight_ref, tile_ref, shifted.at[pair], pair):
            for parity in range(2):
                before = state_ref[pair, parity, :, :, lanes].reshape(INNER * SIDE, 128)
                after = (columns_of(total, parity) + before.astype(F32)).astype(BF16)
                out_ref[pair, parity, :, :, lanes] = after.reshape(INNER, SIDE, 128)


def mixer(block, level, mix_in_ref, mix_out_ref, outs):
    levels = mix_in_ref.shape[1] // 128
    order = [level ^ back for back in range(levels)]
    first = jnp.concatenate([mix_in_ref[block, pl.ds(pl.multiple_of(128 * place, 128), 128), :] for place in order], 0)
    second = [mix_out_ref[block, :, pl.ds(pl.multiple_of(128 * place, 128), 128)] for place in order[:outs]]
    second = jnp.concatenate(second, 1) if outs > 1 else second[0]

    def mix(column):
        hidden = gelu(dot(column, first)).astype(BF16)
        return (column[:, : 128 * outs].astype(F32) + dot(hidden, second)).astype(BF16)

    return mix


def mix_strips_kernel(block, own_ref, one_ref, two_ref, three_ref, mix_in_ref, mix_out_ref, sender_ref, strips_ref, near_ref, far_ref, pair_ref):
    mix = mixer(block, lax.axis_index("level"), mix_in_ref, mix_out_ref, 4)
    column = jnp.concatenate([ref[...].reshape(STRIPS * SIDE, 128) for ref in (own_ref, one_ref, two_ref, three_ref)], 1)
    strips_ref[...] = mix(column).reshape(STRIPS, SIDE, 512)
    address(strips_ref, sender_ref, near_ref, far_ref, pair_ref)


def mix_tiles_kernel(block, own_ref, one_ref, two_ref, three_ref, mix_in_ref, mix_out_ref, inner_ref, out_ref, ring_ref):
    mix = mixer(block, lax.axis_index("level"), mix_in_ref, mix_out_ref, 4)
    for pair in range(HERE // 2):
        for parity in range(2):
            parts = [ref[pair, parity].reshape(INNER * SIDE, 128) for ref in (own_ref, one_ref, two_ref, three_ref)]
            out_ref[pair, parity] = mix(jnp.concatenate(parts, 1)).reshape(INNER, SIDE, 512)
    inner_strips(out_ref, inner_ref, ring_ref)


def last_inner_kernel(block, field_ref, strips_ref, weight_ref, tile_ref, state_ref, mix_in_ref, mix_out_ref, out_ref, shifted):
    mix = mixer(block, lax.axis_index("level"), mix_in_ref, mix_out_ref, 1)
    for pair in range(HERE // 2):
        columns = [], []
        for lanes, total in tile_conv(field_ref, strips_ref, weight_ref, tile_ref, shifted.at[pair], pair):
            for parity in range(2):
                before = state_ref[pair, parity, :, :, lanes].reshape(INNER * SIDE, 128)
                columns[parity].append((columns_of(total, parity) + before.astype(F32)).astype(BF16))
        for parity in range(2):
            mixed = mix(jnp.concatenate(columns[parity], 1))
            out_ref[pair, parity] = mixed.reshape(INNER, SIDE, 128)


def last_border_kernel(block, *refs):
    strips_ref, inner_ref, *received = refs[:7]
    gather_ref, weight_ref, border_ref, state_ref, mix_in_ref, mix_out_ref, tiles_ref, merge_ref, out_ref = refs[7:16]
    mix = mixer(block, lax.axis_index("level"), mix_in_ref, mix_out_ref, 1)
    columns = []
    for lanes, total in border_conv(received, strips_ref, inner_ref, gather_ref, weight_ref, border_ref, *refs[16:]):
        columns.append((total + state_ref[:, :, lanes].reshape(total.shape).astype(F32)).astype(BF16))
    mixed = mix(jnp.concatenate(columns, 1))
    for pair in range(HERE // 2):
        strips = mixed[2 * BORDER * pair : 2 * BORDER * (pair + 1)]
        for group, start in enumerate(STARTS):
            rows = [tiles_ref[pair, parity, start : start + 4].reshape(BORDER, 128) for parity in range(2)]
            merged = dot(merge_ref[group], jnp.concatenate(rows + [strips], 0)).astype(BF16)
            merged = merged.reshape(2, 4, SIDE, 128)
            for tile in range(2):
                out_ref[2 * pair + tile, 4 * group : 4 * group + 4] = merged[tile]


V = pl.BlockSpec(memory_space=pltpu.VMEM)
H = pl.BlockSpec(memory_space=pltpu.HBM)


def call(kernel, name, in_specs, out_specs, out_shape, scratch, args):
    return pl.pallas_call(
        kernel,
        name=name,
        in_specs=in_specs,
        out_specs=out_specs,
        out_shape=out_shape,
        scratch_shapes=scratch,
        compiler_params=pltpu.CompilerParams(vmem_limit_bytes=VMEM_LIMIT),
    )(*(pltpu.with_memory_space_constraint(arg, pltpu.HBM) if spec is H else arg for spec, arg in zip(in_specs, args)))


def arrays(*shapes):
    return [jax.ShapeDtypeStruct(shape, BF16) for shape in shapes]


def strip_shape(features):
    return STRIPS, SIDE, features


def tiles_shape(features):
    return HERE // 2, 2, INNER, SIDE, features


def message_shapes(features):
    return (3, SIDE, features), (3, SIDE, features), (5, SIDE, features)


def border_scratch(features):
    return [pltpu.VMEM((9, STRIPS * SIDE, features), BF16)]


def tile_scratch(features):
    return [pltpu.VMEM((HERE // 2, 4, SIDE, SIDE, features), BF16)]


def send(near, far, to_pair):
    faces = lax.axis_size("face")
    apart = [(i, (i + 2) % faces if i & 2 else (i - 2) % faces) for i in range(faces)]
    from_far = lax.ppermute(far, "face", apart)
    from_near = lax.ppermute(near, "face", [(i, i ^ 2) for i in range(faces)])
    return from_near, from_far, lax.ppermute(to_pair, "face", [(i, i ^ 1) for i in range(faces)])


def receive(sent, beside_near, beside_far):
    near, *beside_near = lax.optimization_barrier((sent[0], *beside_near))
    far, *beside_far = lax.optimization_barrier((sent[1], *beside_far))
    pairs = [(i, i ^ 1) for i in range(lax.axis_size("face"))]
    arrived = near, far, sent[2], lax.ppermute(near, "face", pairs), lax.ppermute(far, "face", pairs)
    return arrived, *beside_near, *beside_far


def from_level(shard, distance):
    levels = lax.axis_size("level")
    return lax.ppermute(shard, "level", [(i, i ^ distance) for i in range(levels)])


def shards(state, conv_weight, mix_in, mix_out, edge_source, corner_source):
    faces = lax.axis_size("face")
    thin = state.shape[-1]
    wide = 4 * thin
    tables = border_table(), tile_table(False), tile_table(True), paired_inner_table(), inner_table()
    border_hbm, plain_hbm, tile_hbm, inner_hbm, ring_hbm = (jnp.asarray(t) for t in tables)
    edges, cornered = edge_source.T, corner_source.T
    edge_scratch = pltpu.SMEM(edges.shape, I32)

    strips, *messages, state, sender = call(
        functools.partial(first_kernel, faces), "first",
        [H, H], [V] * 6,
        arrays(strip_shape(thin), *message_shapes(thin))
        + arrays(state.shape, (11 * SIDE, STRIPS * SIDE)),
        [edge_scratch, pltpu.SMEM((16,), I32), pltpu.SemaphoreType.DMA((2,))],
        (state, edges),
    )
    sent = send(*messages)
    shape_w = (1152, 128), (1152, 128), (1536, 256), (1536, 256)
    gatherer, narrow1, narrow2, wide1, wide2, borders, plain, tiled, inner_places, state_inner = call(
        functools.partial(side_kernel, faces), "side",
        [H] * 8 + [V], [V] * 10,
        arrays((HERE, 80, CANDIDATES), *shape_w, border_hbm.shape, plain_hbm.shape, tile_hbm.shape, inner_hbm.shape, strip_shape(thin)),
        [
            edge_scratch,
            edge_scratch,
            pltpu.VMEM(conv_weight.shape[1:], BF16),
            pltpu.VMEM(ring_hbm.shape, BF16),
            pltpu.SemaphoreType.DMA((8,)),
        ],
        (edges, cornered, conv_weight, border_hbm, plain_hbm, tile_hbm, inner_hbm, ring_hbm, state),
    )

    def border(last, sending, strips, inner_strips, received, weight, residual=()):
        size = strips.shape[-1]
        shapes = [strip_shape(size), *(message_shapes(size) if sending else ())]
        return call(
            functools.partial(border_kernel, last, sending), f"border_{size}_{int(last)}",
            [V] * (11 + len(residual)), [V] * len(shapes),
            arrays(*shapes), border_scratch(size),
            (strips, inner_strips, *received, gatherer, weight, borders, sender, *residual),
        )

    def interior(field, strips, weight, table, keep=False):
        size = field.shape[-1]
        shapes = [tiles_shape(size), strip_shape(size)] + ([tiles_shape(size)] if keep else [])
        return call(
            inner_kernel, f"inner_{size}",
            [V] * 5, [V] * len(shapes), arrays(*shapes), tile_scratch(size),
            (field, strips, weight, table, inner_places),
        )

    received, gatherer = receive(sent, (), (gatherer,))
    inner_edge, *messages = border(False, True, strips, state_inner, received, narrow1)

    sent = send(*messages)
    inner, inner_ring, before = interior(state, strips, wide1, plain, True)
    (field,) = call(
        second_inner_kernel, "inner_second", [V] * 5, [V], arrays(tiles_shape(thin)), tile_scratch(thin),
        (inner, inner_edge, wide2, tiled, before),
    )
    narrow3, narrow4, wide3, wide4, mix_in, mix_out = call(
        weights_kernel, "weights", [H] * 3 + [V], [V] * 6,
        arrays(*shape_w, mix_in.shape, mix_out.shape),
        [pltpu.VMEM(conv_weight.shape[1:], BF16), pltpu.SemaphoreType.DMA((3,))],
        (conv_weight, mix_in, mix_out, inner_edge),
    )
    received, inner_ring, field, mix_in = receive(sent, (inner_ring,), (field, mix_in))
    *received, field = lax.optimization_barrier((*received, field))
    one, three = from_level(field, 1), from_level(field, 3)
    (edge,) = border(True, False, inner_edge, inner_ring, received, narrow2, (strips,))

    parts = [from_level(edge, d) for d in (2, 1, 3)]
    *parts, three = lax.optimization_barrier((*parts, three))
    edge_parts = [edge, parts[1], parts[0], parts[2]]
    fields = [field, one, from_level(three, 1), three]
    strips, *messages = call(
        functools.partial(mix_strips_kernel, 0), "mix_strips",
        [V] * 7, [V] * 4,
        arrays(strip_shape(wide), *message_shapes(wide)), [],
        (*edge_parts, mix_in, mix_out, sender),
    )
    sent = send(*messages)
    field, ring1 = call(
        functools.partial(mix_tiles_kernel, 0), "mix_tiles",
        [V] * 7, [V] * 2, arrays(tiles_shape(wide), strip_shape(wide)), [],
        (*fields, mix_in, mix_out, inner_places),
    )
    received, ring1 = receive(sent, (), (ring1,))
    inner_edge, *messages = border(False, True, strips, ring1, received, narrow3)

    sent = send(*messages)
    inner, inner_ring = interior(field, strips, wide3, tiled)
    tiles = call(
        functools.partial(last_inner_kernel, 1), "last_inner",
        [V] * 7, V, arrays(tiles_shape(thin))[0], tile_scratch(wide),
        (inner, inner_edge, wide4, tiled, field, mix_in, mix_out),
    )
    received, inner_ring, tiles = receive(sent, (inner_ring,), (tiles,))
    return call(
        functools.partial(last_border_kernel, 1), "last_border",
        [V] * 15, V, arrays((HERE, SIDE, SIDE, thin))[0], border_scratch(wide),
        (inner_edge, inner_ring, *received, gatherer, narrow4, borders, strips, mix_in, mix_out, tiles, jnp.asarray(merge_table())),
    )


def solution(mesh):
    return jax.shard_map(
        shards,
        mesh=mesh,
        in_specs=(P(("ens", "face"), None, None, "level"), P(), P(), P(), P(), P()),
        out_specs=P(("ens", "face"), None, None, "level"),
        check_vma=False,
    )
```
